32 devices in a mesh: section: 4 (over y, x), tp: 4 (over z), dp: 2 (over core).
Axes of the slice: x: 2, y: 2, z: 4, core: 2. Of those that a mesh axis runs over, the one named last changes fastest.
Arguments:
- stash: bfloat16 [4, 2, 320, 48, 384], P('section', 'dp', None, 'tp'), may hold values from -24 to 24
- grad_out: bfloat16 [4, 2, 320, 6144], P('section', 'dp', None, 'tp'), may hold values from -6 to 6
- doc_lengths: int32 [4, 2, 8], P('section', 'dp'), may hold values from 1 to 160, 320 in all within a row
Outputs:
- qkv_grad: bfloat16 [4, 2, 320, 48, 384], P('section', 'dp', None, 'tp')
- bias_grad: float32 [4, 48, 384], P('section', 'tp')
The draws below stay inside these ranges and needn't reach their ends.
Inputs may be any that keep to these rules, and one draw needn't show every extreme that they name: `doc_lengths`: the 8 lengths of one micro-batch sum to 320, and in each micro-batch one of them is exactly 160.
All inputs are finite; a program needn't handle non-finite values.
Results may differ from the reference program's by a relative error of at most 0.012.
Values may be sent and summed in bfloat16 or wider, within the bound.
No kernel may reach another device: no remote copies, remote signals or barrier semaphores. Data moves between devices by JAX's collectives and lax.ppermute only.
A program may use at most 64 MiB of HBM per device.

```python
import math
import jax
import jax.numpy as jnp
import numpy as np
from jax import lax

HEADS = 48
HEAD_DIM = 128
L = 320
DOCS = 8
QKV = 384
PIPE = 4
MB = 2
N_DP = 2


def draw_stash(key, part):
    shape = (PIPE, MB, L, HEADS, QKV)
    normal_draw = jax.random.normal(key, shape, jnp.float32)
    return jnp.clip(normal_draw, -24.0, 24.0).astype(jnp.bfloat16)


def steps_of(stream_key, dims, split, least, top_value):
    def one(axis_at, parts):
        draws = jax.random.uniform(jax.random.fold_in(jax.random.fold_in(stream_key, 6), axis_at), (parts,), jnp.float32, least / len(split), top_value / len(split))
        return jnp.repeat(jnp.exp(draws), dims[axis_at] // parts).reshape((-1,) + (1,) * (len(dims) - axis_at - 1))

    level = one(*split[0])
    for cut in split[1:]:
        level = level * one(*cut)
    return level


def length_profile(count, total, reach, slope):
    portions = [(1 << 20) // math.isqrt(rank ** slope) + 1 for rank in range(2, count + 1)]
    rest, holding = total - reach - (count - 1), [1] * (count - 1)
    while rest > 0:
        free = [i for i in range(count - 1) if holding[i] < reach]
        mass, remaining = sum([portions[i] for i in free]), rest
        for i in free:
            extra = min(reach - holding[i], max(1, remaining * portions[i] // mass), rest)
            holding[i] = holding[i] + extra
            rest = rest - extra
    return np.array([reach] + holding)


def ragged_sizes(stream_key, count, total, most, lean):
    if count == 2:
        one = jax.random.randint(stream_key, (), max(1, total - most), min(most, total - 1) + 1)
        return jnp.stack([one, total - one])
    sizes = jnp.asarray(length_profile(count, total, most, lean), jnp.int32)
    pairs = (count - 1) // 2
    source_of, taker = sizes[1:1 + 2 * pairs:2], sizes[2:2 + 2 * pairs:2]
    margin = jnp.minimum(source_of - 1, most - taker)
    moved = jax.random.randint(jax.random.fold_in(stream_key, 1), (pairs,), 0, 1 << 20) % (margin + 1)
    sizes = sizes.at[1:1 + 2 * pairs:2].set(source_of - moved).at[2:2 + 2 * pairs:2].set(taker + moved)
    return sizes[jax.random.permutation(jax.random.fold_in(stream_key, 2), count)]


def centred(own_key, extent, scale, reach, shards=(), held_as=jnp.bfloat16):
    factor_of = steps_of(own_key, extent, shards, -0.22, 0.18) if shards else 1.0
    result = jax.random.normal(own_key, extent, jnp.float32) * scale * factor_of
    return jnp.minimum(jnp.maximum(result, -reach), reach).astype(held_as)


def setup_inputs(seed: int = 0) -> dict:
    keys = jax.random.split(jax.random.key(seed), 4)
    stash = draw_stash(jax.random.fold_in(keys[3], 71), 0)
    grad_out = centred(keys[1], (PIPE, MB, L, HEADS * HEAD_DIM), 1.0, 6.0, ((0, 4), (1, 2), (3, 4)))
    doc_lengths = jax.vmap(lambda own: ragged_sizes(own, DOCS, L, L // 2, 2))(jax.random.split(keys[2], PIPE * MB)).reshape((PIPE, MB, DOCS)).astype(jnp.int32)
    return dict(stash=stash, grad_out=grad_out, doc_lengths=doc_lengths)


def segment_of(lengths, row_count):
    doc_ends = jnp.cumsum(lengths.astype(jnp.int32))
    position = jnp.arange(row_count, dtype=jnp.int32)
    return lax.optimization_barrier(jnp.sum((position[:, None] >= doc_ends[None, :]).astype(jnp.int32), axis=1))

def attention_grads(packed, grad_rows, lengths):
    row_count, head_count, pack_width = packed.shape
    head_size = pack_width // 3
    inv_root = 1.0 / math.sqrt(head_size)
    queries = packed[:, :, :head_size].astype(jnp.float32)
    keys_in = packed[:, :, head_size:2 * head_size].astype(jnp.float32)
    values_in = packed[:, :, 2 * head_size:].astype(jnp.float32)
    grad_heads = grad_rows.reshape(row_count, head_count, head_size).astype(jnp.float32)
    segment = segment_of(lengths, row_count)
    position = jnp.arange(row_count, dtype=jnp.int32)
    allowed = (segment[:, None] == segment[None, :]) & (position[None, :] <= position[:, None])
    scores = jnp.einsum('qhd,khd->hqk', queries, keys_in) * inv_root
    masked = jnp.where(allowed[None], scores, -jnp.inf)
    row_top = lax.optimization_barrier(jnp.max(masked, axis=-1, keepdims=True))
    raised = jnp.exp(masked - row_top)
    attn_prob = raised / lax.optimization_barrier(jnp.sum(raised, axis=-1, keepdims=True))
    prob_low = attn_prob.astype(jnp.bfloat16).astype(jnp.float32)
    attn_out = jnp.einsum('hqk,khd->qhd', prob_low, values_in)
    row_dot = jnp.einsum('qhd,qhd->hq', grad_heads, attn_out)
    prob_grad = jnp.einsum('qhd,khd->hqk', grad_heads, values_in)
    score_grad = attn_prob * (prob_grad - row_dot[:, :, None]) * inv_root
    score_low = score_grad.astype(jnp.bfloat16).astype(jnp.float32)
    query_grad = jnp.einsum('hqk,khd->qhd', score_low, keys_in)
    key_grad = jnp.einsum('hqk,qhd->khd', score_low, queries)
    value_grad = jnp.einsum('hqk,qhd->khd', prob_low, grad_heads)
    return jnp.concatenate([query_grad, key_grad, value_grad], axis=-1)

def one_block(inputs):
    packed, grad_rows, lengths = inputs
    grads = attention_grads(packed, grad_rows, lengths)
    return (grads.astype(jnp.bfloat16), lax.optimization_barrier(jnp.sum(grads, axis=0)))

def reference(stash, grad_out, doc_lengths):
    owned = stash[::-1]
    flat_stash = owned.reshape(PIPE * MB, L, HEADS, QKV)
    flat_grad = grad_out.reshape(PIPE * MB, L, HEADS * HEAD_DIM)
    flat_len = doc_lengths.reshape(PIPE * MB, DOCS)
    grads_low, bias_terms = lax.map(one_block, (flat_stash, flat_grad, flat_len))
    qkv_grad = grads_low.reshape(PIPE, MB, L, HEADS, QKV)
    bias_grad = lax.optimization_barrier(jnp.sum(bias_terms.reshape(PIPE, MB, HEADS, QKV), axis=1)) / N_DP
    return (qkv_grad, bias_grad)
```

```python
import functools
import math

import jax
import jax.numpy as jnp
from jax import lax
from jax.experimental import pallas as pl
from jax.experimental.pallas import tpu as pltpu
from jax.sharding import PartitionSpec as P

MASKED = -1e30


def grads_kernel(lengths_ref, packed_ref, grad_ref, *refs):
    out_ref, bias_ref = refs[-2:]
    row_count = packed_ref.shape[1]
    head_size = packed_ref.shape[2] // 3
    inv_root = 1.0 / math.sqrt(head_size)
    query_at = lax.broadcasted_iota(jnp.int32, (1, row_count), 1)
    doc_start = jnp.zeros((1, row_count), jnp.int32)
    doc_end = jnp.int32(0)
    for doc in range(lengths_ref.shape[0]):
        doc_end = doc_end + lengths_ref[doc]
        doc_start = jnp.where(query_at >= doc_end, doc_end, doc_start)
    key_at = lax.broadcasted_iota(jnp.int32, (row_count, row_count), 0)
    allowed = (key_at >= doc_start) & (key_at <= query_at)

    queries = packed_ref[0, :, :head_size]
    keys_in = packed_ref[0, :, head_size : 2 * head_size]
    values_in = packed_ref[0, :, 2 * head_size :]
    grad_rows = grad_ref[...]
    rows_by_rows = (((1,), (1,)), ((), ()))
    plain = (((1,), (0,)), ((), ()))
    columns = (((0,), (0,)), ((), ()))
    dot = functools.partial(lax.dot_general, preferred_element_type=jnp.float32)

    scores = dot(keys_in, queries, rows_by_rows) * inv_root
    masked = jnp.where(allowed, scores, MASKED)
    raised = jnp.exp(masked - jnp.max(masked, axis=0, keepdims=True))
    prob = raised * (1.0 / jnp.sum(raised, axis=0, keepdims=True))
    prob_low = prob.astype(jnp.bfloat16)
    prob_grad = dot(values_in, grad_rows, rows_by_rows)
    row_dot = jnp.sum(prob_low.astype(jnp.float32) * prob_grad, axis=0, keepdims=True)
    score_low = (prob * (prob_grad - row_dot) * inv_root).astype(jnp.bfloat16)
    grads = (
        dot(score_low, keys_in, columns),
        dot(score_low, queries, plain),
        dot(prob_low, grad_rows, plain),
    )
    for part, grad in enumerate(grads):
        span = slice(part * head_size, (part + 1) * head_size)
        out_ref[0, :, span] = grad.astype(jnp.bfloat16)
        bias_ref[0, :, span] = jnp.sum(grad, axis=0, keepdims=True)


def chunk_grads(packed, grad_rows, lengths, head_count, first_head, previous):
    chunk_heads, row_count, pack_width = packed.shape
    head_size = pack_width // 3
    in_specs = [
        pl.BlockSpec((1, row_count, pack_width), lambda h, _: (h, 0, 0)),
        pl.BlockSpec((row_count, head_size), lambda h, _: (0, first_head + h)),
    ]
    operands = [packed, grad_rows]
    aliases = {}
    if previous is not None:
        in_specs.append(pl.BlockSpec(memory_space=pl.ANY))
        operands.append(previous)
        aliases = {3: 0}
    return pl.pallas_call(
        grads_kernel,
        grid_spec=pltpu.PrefetchScalarGridSpec(
            num_scalar_prefetch=1,
            grid=(chunk_heads,),
            in_specs=in_specs,
            out_specs=[
                pl.BlockSpec((1, row_count, pack_width), lambda h, _: (first_head + h, 0, 0)),
                pl.BlockSpec((1, 1, pack_width), lambda h, _: (h, 0, 0)),
            ],
        ),
        out_shape=[
            jax.ShapeDtypeStruct((head_count, row_count, pack_width), jnp.bfloat16),
            jax.ShapeDtypeStruct((chunk_heads, 1, pack_width), jnp.float32),
        ],
        input_output_aliases=aliases,
        name=f"grads_at_{first_head}",
    )(lengths, *operands)


def chunk_sizes(head_count):
    sizes = []
    rest, size = head_count, 1
    while rest > 0:
        size = min(size, rest)
        sizes.append(size)
        rest -= size
        size *= 3
    return sizes[::-1]


def replica_sum(value, axis):
    count = lax.axis_size(axis)
    if count & (count - 1):
        return lax.psum(value, axis)
    stride = 1
    while stride < count:
        value = value + lax.ppermute(value, axis, [(i, i ^ stride) for i in range(count)])
        stride *= 2
    return value


def body(stash, grad_out, doc_lengths):
    by_head = jnp.transpose(stash[0, 0], (1, 0, 2))
    head_count = by_head.shape[0]
    section_count = lax.axis_size("section")
    mirror = [(i, section_count - 1 - i) for i in range(section_count)]
    sizes = chunk_sizes(head_count)
    firsts = [sum(sizes[:i]) for i in range(len(sizes))]
    arrived = []
    for index, (first, size) in enumerate(zip(firsts, sizes)):
        with jax.named_scope(f"chunk{index}"):
            arrived.append(lax.ppermute(by_head[first : first + size], "section", mirror))
    grads, bias_parts = None, []
    for first, packed in zip(firsts, arrived):
        grads, bias = chunk_grads(
            packed, grad_out[0, 0], doc_lengths[0, 0], head_count, first, grads
        )
        bias_parts.append(bias)
    bias_total = replica_sum(jnp.concatenate(bias_parts, axis=0), "dp")
    bias_grad = jnp.transpose(bias_total / lax.axis_size("dp"), (1, 0, 2))
    return (jnp.transpose(grads, (1, 0, 2))[None, None], bias_grad)


def solution(mesh):
    in_specs = (
        P("section", "dp", None, "tp", None),
        P("section", "dp", None, "tp"),
        P("section", "dp", None),
    )
    out_specs = (P("section", "dp", None, "tp", None), P("section", "tp", None))
    return jax.shard_map(body, mesh=mesh, in_specs=in_specs, out_specs=out_specs, check_vma=False)
```

```python
import functools
import math

import jax
import jax.numpy as jnp
from jax import lax
from jax.experimental import pallas as pl
from jax.experimental.pallas import tpu as pltpu
from jax.sharding import PartitionSpec as P

MASKED = -1e30
KERNEL_VMEM = 16 * 1024 * 1024


def doc_starts(lengths_ref, row_count):
    query_at = lax.broadcasted_iota(jnp.int32, (1, row_count), 1)
    doc_start = jnp.zeros((1, row_count), jnp.int32)
    doc_end = jnp.int32(0)
    for doc in range(lengths_ref.shape[0]):
        doc_end = doc_end + lengths_ref[doc]
        doc_start = jnp.where(query_at >= doc_end, doc_end, doc_start)
    return doc_start


def head_grads(packed, grad_rows, doc_start):
    row_count, pack_width = packed.shape
    head_size = pack_width // 3
    inv_root = 1.0 / math.sqrt(head_size)
    query_at = lax.broadcasted_iota(jnp.int32, (1, row_count), 1)
    key_at = lax.broadcasted_iota(jnp.int32, (row_count, row_count), 0)
    allowed = (key_at >= doc_start) & (key_at <= query_at)
    queries = packed[:, :head_size]
    keys_in = packed[:, head_size : 2 * head_size]
    values_in = packed[:, 2 * head_size :]
    rows_by_rows = (((1,), (1,)), ((), ()))
    plain = (((1,), (0,)), ((), ()))
    columns = (((0,), (0,)), ((), ()))
    dot = functools.partial(lax.dot_general, preferred_element_type=jnp.float32)

    scores = dot(keys_in, queries, rows_by_rows) * inv_root
    masked = jnp.where(allowed, scores, MASKED)
    raised = jnp.exp(masked - jnp.max(masked, axis=0, keepdims=True))
    prob = raised * (1.0 / jnp.sum(raised, axis=0, keepdims=True))
    prob_low = prob.astype(jnp.bfloat16)
    prob_grad = dot(values_in, grad_rows, rows_by_rows)
    row_dot = jnp.sum(prob_low.astype(jnp.float32) * prob_grad, axis=0, keepdims=True)
    score_low = (prob * (prob_grad - row_dot) * inv_root).astype(jnp.bfloat16)
    return (
        dot(score_low, keys_in, columns),
        dot(score_low, queries, plain),
        dot(prob_low, grad_rows, plain),
    )


def write_head(grads, out_ref, out_head, bias_ref, bias_head):
    for part, grad in enumerate(grads):
        head_size = grad.shape[1]
        span = slice(part * head_size, (part + 1) * head_size)
        out_ref[out_head, :, span] = grad.astype(jnp.bfloat16)
        bias_ref[bias_head, :, span] = jnp.sum(grad, axis=0, keepdims=True)


def chunk_kernel(lengths_ref, packed_ref, grad_ref, *refs, first_head):
    out_ref, bias_ref = refs[-2:]
    row_count, pack_width = packed_ref.shape[1:]
    head_size = pack_width // 3
    head = pl.program_id(0)
    grad_at = pl.multiple_of((first_head + head) * head_size, head_size)
    grads = head_grads(
        packed_ref[head], grad_ref[:, pl.ds(grad_at, head_size)], doc_starts(lengths_ref, row_count)
    )
    write_head(grads, out_ref, 0, bias_ref, head)


def last_kernel(lengths_ref, packed_ref, grad_ref, *refs):
    bias_parts, (out_ref, bias_ref) = refs[:-2], refs[-2:]
    row_count, pack_width = packed_ref.shape[1:]
    head_size = pack_width // 3
    head_at = 0
    for part_ref in bias_parts:
        bias_ref[head_at : head_at + part_ref.shape[0]] = part_ref[...]
        head_at += part_ref.shape[0]
    grads = head_grads(
        packed_ref[0],
        grad_ref[:, head_at * head_size : (head_at + 1) * head_size],
        doc_starts(lengths_ref, row_count),
    )
    write_head(grads, out_ref, 0, bias_ref, head_at)


def store_kernel(head_ref, _, out_ref, semaphore):
    at = out_ref.shape[0] - head_ref.shape[0]
    copy = pltpu.make_async_copy(head_ref, out_ref.at[pl.ds(at, head_ref.shape[0])], semaphore)
    copy.start()
    copy.wait()


def in_vmem(array):
    return pltpu.with_memory_space_constraint(array, pltpu.VMEM)


VMEM_SPEC = pl.BlockSpec(memory_space=pltpu.VMEM)
SMEM_SPEC = pl.BlockSpec(memory_space=pltpu.SMEM)
ANY_SPEC = pl.BlockSpec(memory_space=pl.ANY)


def chunk_grads(packed, grad_rows, lengths, head_count, first_head, previous):
    chunk_heads, row_count, pack_width = packed.shape
    in_specs = [SMEM_SPEC, VMEM_SPEC, VMEM_SPEC]
    operands = [lengths, in_vmem(packed), in_vmem(grad_rows)]
    aliases = {}
    if previous is not None:
        in_specs.append(ANY_SPEC)
        operands.append(previous)
        aliases = {3: 0}
    return pl.pallas_call(
        functools.partial(chunk_kernel, first_head=first_head),
        grid=(chunk_heads,),
        in_specs=in_specs,
        out_specs=[
            pl.BlockSpec((1, row_count, pack_width), lambda h: (first_head + h, 0, 0)),
            VMEM_SPEC,
        ],
        out_shape=[
            jax.ShapeDtypeStruct((head_count, row_count, pack_width), jnp.bfloat16),
            pltpu.VMEM((chunk_heads, 1, pack_width), jnp.float32),
        ],
        input_output_aliases=aliases,
        compiler_params=pltpu.CompilerParams(vmem_limit_bytes=KERNEL_VMEM),
    )(*operands)


def last_grads(packed, grad_rows, lengths, bias_parts):
    _, row_count, pack_width = packed.shape
    head_count = 1 + sum(part.shape[0] for part in bias_parts)
    return pl.pallas_call(
        last_kernel,
        in_specs=[SMEM_SPEC] + [VMEM_SPEC] * (2 + len(bias_parts)),
        out_specs=[VMEM_SPEC, VMEM_SPEC],
        out_shape=[
            pltpu.VMEM((1, row_count, pack_width), jnp.bfloat16),
            pltpu.VMEM((head_count, 1, pack_width), jnp.float32),
        ],
        compiler_params=pltpu.CompilerParams(vmem_limit_bytes=KERNEL_VMEM),
        name="last_grads",
    )(lengths, in_vmem(packed), in_vmem(grad_rows), *[in_vmem(part) for part in bias_parts])


def store_last(head, grads):
    return pl.pallas_call(
        store_kernel,
        in_specs=[VMEM_SPEC, ANY_SPEC],
        out_specs=ANY_SPEC,
        out_shape=jax.ShapeDtypeStruct(grads.shape, grads.dtype),
        scratch_shapes=[pltpu.SemaphoreType.DMA],
        input_output_aliases={1: 0},
        compiler_params=pltpu.CompilerParams(vmem_limit_bytes=KERNEL_VMEM),
        name="store_last",
    )(in_vmem(head), grads)


def chunk_sizes(head_count):
    tail = [2, 1, 1]
    if head_count < sum(tail) + 2:
        return [1] * head_count
    return [1, head_count - sum(tail) - 1] + tail


def replica_sum(value, axis):
    count = lax.axis_size(axis)
    if count & (count - 1):
        return lax.psum(value, axis)
    stride = 1
    while stride < count:
        value = value + lax.ppermute(value, axis, [(i, i ^ stride) for i in range(count)])
        stride *= 2
    return value


def body(stash, grad_out, doc_lengths):
    by_head = jnp.transpose(stash[0, 0], (1, 0, 2))
    head_count = by_head.shape[0]
    section_count = lax.axis_size("section")
    mirror = [(i, section_count - 1 - i) for i in range(section_count)]
    sizes = chunk_sizes(head_count)
    firsts = [sum(sizes[:i]) for i in range(len(sizes))]
    arrived = []
    for first, size in zip(firsts, sizes):
        piece, by_head = lax.optimization_barrier((by_head[first : first + size], by_head))
        arrived.append(lax.ppermute(piece, "section", mirror))
    grad_rows, lengths = grad_out[0, 0], doc_lengths[0, 0]
    grads, bias_parts = None, []
    for first, packed in zip(firsts[:-1], arrived):
        grads, bias = chunk_grads(packed, grad_rows, lengths, head_count, first, grads)
        bias_parts.append(bias)
    last, bias_own = last_grads(arrived[-1], grad_rows, lengths, bias_parts)
    bias_total = replica_sum(bias_own, "dp")
    grads = store_last(last, grads)
    bias_grad = jnp.transpose(bias_total / lax.axis_size("dp"), (1, 0, 2))
    return (jnp.transpose(grads, (1, 0, 2))[None, None], bias_grad)


def solution(mesh):
    in_specs = (
        P("section", "dp", None, "tp", None),
        P("section", "dp", None, "tp"),
        P("section", "dp", None),
    )
    out_specs = (P("section", "dp", None, "tp", None), P("section", "tp", None))
    return jax.shard_map(body, mesh=mesh, in_specs=in_specs, out_specs=out_specs, check_vma=False)
```

```python
import functools
import math

import jax
import jax.numpy as jnp
from jax import lax
from jax.experimental import pallas as pl
from jax.experimental.pallas import tpu as pltpu
from jax.sharding import PartitionSpec as P

MASKED = -1e30
TILE = 128
KERNEL_VMEM = 16 * 1024 * 1024


def doc_starts(lengths_ref, row_count):
    query_at = lax.broadcasted_iota(jnp.int32, (1, row_count), 1)
    doc_start = jnp.zeros((1, row_count), jnp.int32)
    doc_end = jnp.int32(0)
    for doc in range(lengths_ref.shape[0]):
        doc_end = doc_end + lengths_ref[doc]
        doc_start = jnp.where(query_at >= doc_end, doc_end, doc_start)
    return doc_start


ROWS_BY_ROWS = (((1,), (1,)), ((), ()))
PLAIN = (((1,), (0,)), ((), ()))
COLUMNS = (((0,), (0,)), ((), ()))
dot = functools.partial(lax.dot_general, preferred_element_type=jnp.float32)


def split_pack(packed):
    head_size = packed.shape[1] // 3
    return (
        packed[:, :head_size],
        packed[:, head_size : 2 * head_size],
        packed[:, 2 * head_size :],
    )


def tile_weights(queries, keys_in, values_in, grad_rows, doc_start, first_query):
    inv_root = 1.0 / math.sqrt(queries.shape[1])
    shape = (keys_in.shape[0], queries.shape[0])
    query_at = first_query + lax.broadcasted_iota(jnp.int32, (1, shape[1]), 1)
    key_at = lax.broadcasted_iota(jnp.int32, shape, 0)
    allowed = (key_at >= doc_start) & (key_at <= query_at)
    scores = dot(keys_in, queries, ROWS_BY_ROWS) * inv_root
    masked = jnp.where(allowed, scores, MASKED)
    raised = jnp.exp(masked - jnp.max(masked, axis=0, keepdims=True))
    prob = raised * (1.0 / jnp.sum(raised, axis=0, keepdims=True))
    prob_low = prob.astype(jnp.bfloat16)
    prob_grad = dot(values_in, grad_rows, ROWS_BY_ROWS)
    row_dot = jnp.sum(prob_low.astype(jnp.float32) * prob_grad, axis=0, keepdims=True)
    score_low = (prob * (prob_grad - row_dot) * inv_root).astype(jnp.bfloat16)
    return prob_low, score_low


def head_grads(packed, grad_rows, doc_start):
    queries, keys_in, values_in = split_pack(packed)
    prob_low, score_low = tile_weights(queries, keys_in, values_in, grad_rows, doc_start, 0)
    return (
        dot(score_low, keys_in, COLUMNS),
        dot(score_low, queries, PLAIN),
        dot(prob_low, grad_rows, PLAIN),
    )


def write_head(grads, out_ref, out_head, bias_ref, bias_head):
    for part, grad in enumerate(grads):
        head_size = grad.shape[1]
        span = slice(part * head_size, (part + 1) * head_size)
        out_ref[out_head, :, span] = grad.astype(jnp.bfloat16)
        bias_ref[bias_head, :, span] = jnp.sum(grad, axis=0, keepdims=True)


def chunk_kernel(lengths_ref, packed_ref, grad_ref, *refs, first_head):
    out_ref, bias_ref = refs[-2:]
    row_count, pack_width = packed_ref.shape[1:]
    head_size = pack_width // 3
    head = pl.program_id(0)
    grad_at = pl.multiple_of((first_head + head) * head_size, head_size)
    grads = head_grads(
        packed_ref[head], grad_ref[:, pl.ds(grad_at, head_size)], doc_starts(lengths_ref, row_count)
    )
    write_head(grads, out_ref, 0, bias_ref, head)


def early_kernel(lengths_ref, early_ref, grad_ref, _, query_ref, sums_ref, bias_ref, *, head):
    row_count, pack_width = early_ref.shape[1:]
    head_size = pack_width // 3
    queries, keys_in, values_in = split_pack(early_ref[0])
    grad_rows = grad_ref[:row_count, head * head_size : (head + 1) * head_size]
    doc_start = doc_starts(lengths_ref, row_count)
    tiles = [slice(at, at + TILE) for at in range(0, row_count, TILE)]
    key_grads, value_grads = [0.0] * len(tiles), [0.0] * len(tiles)
    bias = jnp.zeros((1, head_size), jnp.float32)
    for index, tile in enumerate(tiles):
        seen = slice(0, tile.stop)
        prob_low, score_low = tile_weights(
            queries[tile], keys_in[seen], values_in[seen], grad_rows[tile], doc_start[:, tile], tile.start
        )
        query_grad = dot(score_low, keys_in[seen], COLUMNS)
        query_ref[tile] = query_grad.astype(jnp.bfloat16)
        bias += jnp.sum(query_grad, axis=0, keepdims=True)
        for past in range(index + 1):
            key_grads[past] += dot(score_low[tiles[past]], queries[tile], PLAIN)
            value_grads[past] += dot(prob_low[tiles[past]], grad_rows[tile], PLAIN)
    bias_ref[...] = bias
    for index, tile in enumerate(tiles):
        sums_ref[tile, :head_size] = key_grads[index]
        sums_ref[tile, head_size:] = value_grads[index]


def late_kernel(lengths_ref, early_ref, late_ref, grad_ref, query_ref, sums_ref, early_bias_ref, *refs):
    bias_parts, (out_ref, bias_ref) = refs[:-2], refs[-2:]
    split = early_ref.shape[1]
    row_count = split + late_ref.shape[1]
    head_size = early_ref.shape[2] // 3
    head = sum(part_ref.shape[0] for part_ref in bias_parts)
    queries = late_ref[0, :, :head_size]
    grad_rows = grad_ref[split:, head * head_size : (head + 1) * head_size]
    keys_in, values_in = (
        jnp.concatenate([ref[0, :, part * head_size : (part + 1) * head_size] for ref in (early_ref, late_ref)], axis=0)
        for part in (1, 2)
    )
    prob_low, score_low = tile_weights(
        queries, keys_in, values_in, grad_rows, doc_starts(lengths_ref, row_count)[:, split:], split
    )
    query_grad = dot(score_low, keys_in, COLUMNS)
    out_ref[0, :split, :head_size] = query_ref[...]
    out_ref[0, split:, :head_size] = query_grad.astype(jnp.bfloat16)
    bias_ref[head, :, :head_size] = early_bias_ref[...] + jnp.sum(query_grad, axis=0, keepdims=True)
    added = (dot(score_low, queries, PLAIN), dot(prob_low, grad_rows, PLAIN))
    for part, late in enumerate(added):
        span = slice((part + 1) * head_size, (part + 2) * head_size)
        early = sums_ref[:, part * head_size : (part + 1) * head_size] + late[:split]
        out_ref[0, :split, span] = early.astype(jnp.bfloat16)
        out_ref[0, split:, span] = late[split:].astype(jnp.bfloat16)
        bias_ref[head, :, span] = jnp.sum(early, axis=0, keepdims=True) + jnp.sum(
            late[split:], axis=0, keepdims=True
        )
    head_at = 0
    for part_ref in bias_parts:
        bias_ref[head_at : head_at + part_ref.shape[0]] = part_ref[...]
        head_at += part_ref.shape[0]


def store_kernel(head_ref, _, out_ref, semaphore):
    at = out_ref.shape[0] - head_ref.shape[0]
    copy = pltpu.make_async_copy(head_ref, out_ref.at[pl.ds(at, head_ref.shape[0])], semaphore)
    copy.start()
    copy.wait()


def in_vmem(array):
    return pltpu.with_memory_space_constraint(array, pltpu.VMEM)


VMEM_SPEC = pl.BlockSpec(memory_space=pltpu.VMEM)
SMEM_SPEC = pl.BlockSpec(memory_space=pltpu.SMEM)
ANY_SPEC = pl.BlockSpec(memory_space=pl.ANY)


def chunk_grads(packed, grad_rows, lengths, head_count, first_head, previous):
    chunk_heads, row_count, pack_width = packed.shape
    in_specs = [SMEM_SPEC, VMEM_SPEC, VMEM_SPEC]
    operands = [lengths, in_vmem(packed), in_vmem(grad_rows)]
    aliases = {}
    if previous is not None:
        in_specs.append(ANY_SPEC)
        operands.append(previous)
        aliases = {3: 0}
    return pl.pallas_call(
        functools.partial(chunk_kernel, first_head=first_head),
        grid=(chunk_heads,),
        in_specs=in_specs,
        out_specs=[
            pl.BlockSpec((1, row_count, pack_width), lambda h: (first_head + h, 0, 0)),
            VMEM_SPEC,
        ],
        out_shape=[
            jax.ShapeDtypeStruct((head_count, row_count, pack_width), jnp.bfloat16),
            pltpu.VMEM((chunk_heads, 1, pack_width), jnp.float32),
        ],
        input_output_aliases=aliases,
        compiler_params=pltpu.CompilerParams(vmem_limit_bytes=KERNEL_VMEM),
    )(*operands)


def early_grads(packed, grad_rows, lengths, head, after):
    _, row_count, pack_width = packed.shape
    head_size = pack_width // 3
    return pl.pallas_call(
        functools.partial(early_kernel, head=head),
        in_specs=[SMEM_SPEC] + [VMEM_SPEC] * 3,
        out_specs=[VMEM_SPEC] * 3,
        out_shape=[
            pltpu.VMEM((row_count, head_size), jnp.bfloat16),
            pltpu.VMEM((row_count, 2 * head_size), jnp.float32),
            pltpu.VMEM((1, head_size), jnp.float32),
        ],
        compiler_params=pltpu.CompilerParams(vmem_limit_bytes=KERNEL_VMEM),
        name="early_grads",
    )(lengths, in_vmem(packed), in_vmem(grad_rows), in_vmem(after))


def late_grads(early, late, grad_rows, lengths, started, bias_parts):
    head_count = 1 + sum(part.shape[0] for part in bias_parts)
    row_count, pack_width = grad_rows.shape[0], early.shape[2]
    operands = [early, late, grad_rows, *started, *bias_parts]
    return pl.pallas_call(
        late_kernel,
        in_specs=[SMEM_SPEC] + [VMEM_SPEC] * len(operands),
        out_specs=[VMEM_SPEC, VMEM_SPEC],
        out_shape=[
            pltpu.VMEM((1, row_count, pack_width), jnp.bfloat16),
            pltpu.VMEM((head_count, 1, pack_width), jnp.float32),
        ],
        compiler_params=pltpu.CompilerParams(vmem_limit_bytes=KERNEL_VMEM),
        name="late_grads",
    )(lengths, *[in_vmem(operand) for operand in operands])


def store_last(head, grads):
    return pl.pallas_call(
        store_kernel,
        in_specs=[VMEM_SPEC, ANY_SPEC],
        out_specs=ANY_SPEC,
        out_shape=jax.ShapeDtypeStruct(grads.shape, grads.dtype),
        scratch_shapes=[pltpu.SemaphoreType.DMA],
        input_output_aliases={1: 0},
        compiler_params=pltpu.CompilerParams(vmem_limit_bytes=KERNEL_VMEM),
        name="store_last",
    )(in_vmem(head), grads)


def chunk_sizes(head_count):
    tail = [2, 1]
    if head_count < sum(tail) + 2:
        return [1] * head_count
    return [1, head_count - sum(tail) - 1] + tail


def replica_sum(value, axis):
    count = lax.axis_size(axis)
    if count & (count - 1):
        return lax.psum(value, axis)
    stride = 1
    while stride < count:
        value = value + lax.ppermute(value, axis, [(i, i ^ stride) for i in range(count)])
        stride *= 2
    return value


def body(stash, grad_out, doc_lengths):
    by_head = jnp.transpose(stash[0, 0], (1, 0, 2))
    head_count = by_head.shape[0]
    section_count = lax.axis_size("section")
    mirror = [(i, section_count - 1 - i) for i in range(section_count)]
    row_count = by_head.shape[1]
    split = (row_count - 1) // TILE * TILE
    last = head_count - 1
    sizes = chunk_sizes(last)
    firsts = [sum(sizes[:i]) for i in range(len(sizes))]
    pieces = [(slice(first, first + size), slice(None)) for first, size in zip(firsts, sizes)]
    pieces += [(slice(last, None), slice(0, split)), (slice(last, None), slice(split, None))]
    grad_rows, lengths = grad_out[0, 0], doc_lengths[0, 0]
    arrived = []
    for piece in pieces:
        packed, by_head = lax.optimization_barrier((by_head[piece], by_head))
        arrived.append(lax.ppermute(packed, "section", mirror))
    grads, bias_parts = None, []
    for first, packed in zip(firsts, arrived):
        grads, bias = chunk_grads(packed, grad_rows, lengths, head_count, first, grads)
        bias_parts.append(bias)
    early, late = arrived[-2:]
    started = early_grads(early, grad_rows, lengths, last, bias_parts[-1])
    final, bias_own = late_grads(early, late, grad_rows, lengths, started, bias_parts)
    bias_total = replica_sum(bias_own, "dp")
    grads = store_last(final, grads)
    bias_grad = jnp.transpose(bias_total / lax.axis_size("dp"), (1, 0, 2))
    return (jnp.transpose(grads, (1, 0, 2))[None, None], bias_grad)


def solution(mesh):
    in_specs = (
        P("section", "dp", None, "tp", None),
        P("section", "dp", None, "tp"),
        P("section", "dp", None),
    )
    out_specs = (P("section", "dp", None, "tp", None), P("section", "tp", None))
    return jax.shard_map(body, mesh=mesh, in_specs=in_specs, out_specs=out_specs, check_vma=False)
```

```python
import functools
import math

import jax
import jax.numpy as jnp
from jax import lax
from jax.experimental import pallas as pl
from jax.experimental.pallas import tpu as pltpu
from jax.sharding import PartitionSpec as P

MASKED = -1e30
TILE = 128
KERNEL_VMEM = 16 * 1024 * 1024


def doc_starts(lengths_ref, row_count):
    query_at = lax.broadcasted_iota(jnp.int32, (1, row_count), 1)
    doc_start = jnp.zeros((1, row_count), jnp.int32)
    doc_end = jnp.int32(0)
    for doc in range(lengths_ref.shape[0]):
        doc_end = doc_end + lengths_ref[doc]
        doc_start = jnp.where(query_at >= doc_end, doc_end, doc_start)
    return doc_start


ROWS_BY_ROWS = (((1,), (1,)), ((), ()))
PLAIN = (((1,), (0,)), ((), ()))
COLUMNS = (((0,), (0,)), ((), ()))
dot = functools.partial(lax.dot_general, preferred_element_type=jnp.float32)


def split_pack(packed):
    head_size = packed.shape[1] // 3
    return (
        packed[:, :head_size],
        packed[:, head_size : 2 * head_size],
        packed[:, 2 * head_size :],
    )


def tile_weights(queries, keys_in, values_in, grad_rows, doc_start, first_query):
    inv_root = 1.0 / math.sqrt(queries.shape[1])
    shape = (keys_in.shape[0], queries.shape[0])
    query_at = first_query + lax.broadcasted_iota(jnp.int32, (1, shape[1]), 1)
    key_at = lax.broadcasted_iota(jnp.int32, shape, 0)
    allowed = (key_at >= doc_start) & (key_at <= query_at)
    scores = dot(keys_in, queries, ROWS_BY_ROWS) * inv_root
    masked = jnp.where(allowed, scores, MASKED)
    raised = jnp.exp(masked - jnp.max(masked, axis=0, keepdims=True))
    prob = raised * (1.0 / jnp.sum(raised, axis=0, keepdims=True))
    prob_low = prob.astype(jnp.bfloat16)
    prob_grad = dot(values_in, grad_rows, ROWS_BY_ROWS)
    row_dot = jnp.sum(prob_low.astype(jnp.float32) * prob_grad, axis=0, keepdims=True)
    score_low = (prob * (prob_grad - row_dot) * inv_root).astype(jnp.bfloat16)
    return prob_low, score_low


def head_grads(packed, grad_rows, doc_start):
    queries, keys_in, values_in = split_pack(packed)
    prob_low, score_low = tile_weights(queries, keys_in, values_in, grad_rows, doc_start, 0)
    return (
        dot(score_low, keys_in, COLUMNS),
        dot(score_low, queries, PLAIN),
        dot(prob_low, grad_rows, PLAIN),
    )


def write_head(grads, out_ref, out_head, bias_ref, bias_head):
    for part, grad in enumerate(grads):
        head_size = grad.shape[1]
        span = slice(part * head_size, (part + 1) * head_size)
        out_ref[out_head, :, span] = grad.astype(jnp.bfloat16)
        bias_ref[bias_head, :, span] = jnp.sum(grad, axis=0, keepdims=True)


def chunk_kernel(packed_ref, grad_ref, start_ref, _, out_ref, bias_ref, *, first_head):
    head_size = packed_ref.shape[2] // 3
    head = pl.program_id(0)
    grad_at = pl.multiple_of((first_head + head) * head_size, head_size)
    grads = head_grads(packed_ref[head], grad_ref[:, pl.ds(grad_at, head_size)], start_ref[...])
    write_head(grads, out_ref, 0, bias_ref, head)


def first_kernel(lengths_ref, packed_ref, grad_ref, out_ref, bias_ref, start_ref):
    @pl.when(pl.program_id(0) == 0)
    def _():
        start_ref[...] = doc_starts(lengths_ref, packed_ref.shape[1])

    chunk_kernel(packed_ref, grad_ref, start_ref, None, out_ref, bias_ref, first_head=0)


def early_kernel(early_ref, grad_ref, start_ref, _, query_ref, sums_ref, bias_ref, *, head):
    row_count, pack_width = early_ref.shape[1:]
    head_size = pack_width // 3
    queries, keys_in, values_in = split_pack(early_ref[0])
    grad_rows = grad_ref[:row_count, head * head_size : (head + 1) * head_size]
    doc_start = start_ref[...]
    tiles = [slice(at, at + TILE) for at in range(0, row_count, TILE)]
    key_grads, value_grads = [0.0] * len(tiles), [0.0] * len(tiles)
    bias = jnp.zeros((1, head_size), jnp.float32)
    for index, tile in enumerate(tiles):
        seen = slice(0, tile.stop)
        prob_low, score_low = tile_weights(
            queries[tile], keys_in[seen], values_in[seen], grad_rows[tile], doc_start[:, tile], tile.start
        )
        query_grad = dot(score_low, keys_in[seen], COLUMNS)
        query_ref[tile] = query_grad.astype(jnp.bfloat16)
        bias += jnp.sum(query_grad, axis=0, keepdims=True)
        for past in range(index + 1):
            key_grads[past] += dot(score_low[tiles[past]], queries[tile], PLAIN)
            value_grads[past] += dot(prob_low[tiles[past]], grad_rows[tile], PLAIN)
    bias_ref[...] = bias
    for index, tile in enumerate(tiles):
        sums_ref[tile, :head_size] = key_grads[index]
        sums_ref[tile, head_size:] = value_grads[index]


def late_kernel(early_ref, late_ref, grad_ref, start_ref, query_ref, sums_ref, early_bias_ref, *refs):
    bias_parts, (out_ref, bias_ref) = refs[:-2], refs[-2:]
    split = early_ref.shape[1]
    head_size = early_ref.shape[2] // 3
    head = sum(part_ref.shape[0] for part_ref in bias_parts)
    queries = late_ref[0, :, :head_size]
    grad_rows = grad_ref[split:, head * head_size : (head + 1) * head_size]
    keys_in, values_in = (
        jnp.concatenate([ref[0, :, part * head_size : (part + 1) * head_size] for ref in (early_ref, late_ref)], axis=0)
        for part in (1, 2)
    )
    prob_low, score_low = tile_weights(
        queries, keys_in, values_in, grad_rows, start_ref[:, split:], split
    )
    query_grad = dot(score_low, keys_in, COLUMNS)
    out_ref[0, :split, :head_size] = query_ref[...]
    out_ref[0, split:, :head_size] = query_grad.astype(jnp.bfloat16)
    bias_ref[head, :, :head_size] = early_bias_ref[...] + jnp.sum(query_grad, axis=0, keepdims=True)
    added = (dot(score_low, queries, PLAIN), dot(prob_low, grad_rows, PLAIN))
    for part, late in enumerate(added):
        span = slice((part + 1) * head_size, (part + 2) * head_size)
        early = sums_ref[:, part * head_size : (part + 1) * head_size] + late[:split]
        out_ref[0, :split, span] = early.astype(jnp.bfloat16)
        out_ref[0, split:, span] = late[split:].astype(jnp.bfloat16)
        bias_ref[head, :, span] = jnp.sum(early, axis=0, keepdims=True) + jnp.sum(
            late[split:], axis=0, keepdims=True
        )
    head_at = 0
    for part_ref in bias_parts:
        bias_ref[head_at : head_at + part_ref.shape[0]] = part_ref[...]
        head_at += part_ref.shape[0]


def store_kernel(head_ref, _, out_ref, semaphore):
    at = out_ref.shape[0] - head_ref.shape[0]
    copy = pltpu.make_async_copy(head_ref, out_ref.at[pl.ds(at, head_ref.shape[0])], semaphore)
    copy.start()
    copy.wait()


def in_vmem(array):
    return pltpu.with_memory_space_constraint(array, pltpu.VMEM)


VMEM_SPEC = pl.BlockSpec(memory_space=pltpu.VMEM)
SMEM_SPEC = pl.BlockSpec(memory_space=pltpu.SMEM)
ANY_SPEC = pl.BlockSpec(memory_space=pl.ANY)


def chunk_grads(packed, grad_rows, lengths, head_count, first_head, start_row, previous):
    chunk_heads, row_count, pack_width = packed.shape
    blocks = [in_vmem(packed), in_vmem(grad_rows)]
    out_specs = [
        pl.BlockSpec((1, row_count, pack_width), lambda h: (first_head + h, 0, 0)),
        VMEM_SPEC,
    ]
    out_shape = [
        jax.ShapeDtypeStruct((head_count, row_count, pack_width), jnp.bfloat16),
        pltpu.VMEM((chunk_heads, 1, pack_width), jnp.float32),
    ]
    options = dict(
        grid=(chunk_heads,),
        compiler_params=pltpu.CompilerParams(vmem_limit_bytes=KERNEL_VMEM),
        name=f"grads_at_{first_head}",
    )
    if previous is None:
        return pl.pallas_call(
            first_kernel,
            in_specs=[SMEM_SPEC, VMEM_SPEC, VMEM_SPEC],
            out_specs=out_specs + [VMEM_SPEC],
            out_shape=out_shape + [pltpu.VMEM((1, row_count), jnp.int32)],
            **options,
        )(lengths, *blocks)
    grads, bias = pl.pallas_call(
        functools.partial(chunk_kernel, first_head=first_head),
        in_specs=[VMEM_SPEC, VMEM_SPEC, VMEM_SPEC, ANY_SPEC],
        out_specs=out_specs,
        out_shape=out_shape,
        input_output_aliases={3: 0},
        **options,
    )(*blocks, in_vmem(start_row), previous)
    return grads, bias, start_row


def early_grads(packed, grad_rows, start_row, head, after):
    _, row_count, pack_width = packed.shape
    head_size = pack_width // 3
    return pl.pallas_call(
        functools.partial(early_kernel, head=head),
        in_specs=[VMEM_SPEC] * 4,
        out_specs=[VMEM_SPEC] * 3,
        out_shape=[
            pltpu.VMEM((row_count, head_size), jnp.bfloat16),
            pltpu.VMEM((row_count, 2 * head_size), jnp.float32),
            pltpu.VMEM((1, head_size), jnp.float32),
        ],
        compiler_params=pltpu.CompilerParams(vmem_limit_bytes=KERNEL_VMEM),
        name="early_grads",
    )(in_vmem(packed), in_vmem(grad_rows), in_vmem(start_row), in_vmem(after))


def late_grads(early, late, grad_rows, start_row, started, bias_parts):
    head_count = 1 + sum(part.shape[0] for part in bias_parts)
    row_count, pack_width = grad_rows.shape[0], early.shape[2]
    operands = [early, late, grad_rows, start_row, *started, *bias_parts]
    return pl.pallas_call(
        late_kernel,
        in_specs=[VMEM_SPEC] * len(operands),
        out_specs=[VMEM_SPEC, VMEM_SPEC],
        out_shape=[
            pltpu.VMEM((1, row_count, pack_width), jnp.bfloat16),
            pltpu.VMEM((head_count, 1, pack_width), jnp.float32),
        ],
        compiler_params=pltpu.CompilerParams(vmem_limit_bytes=KERNEL_VMEM),
        name="late_grads",
    )(*[in_vmem(operand) for operand in operands])


def store_last(head, grads):
    return pl.pallas_call(
        store_kernel,
        in_specs=[VMEM_SPEC, ANY_SPEC],
        out_specs=ANY_SPEC,
        out_shape=jax.ShapeDtypeStruct(grads.shape, grads.dtype),
        scratch_shapes=[pltpu.SemaphoreType.DMA],
        input_output_aliases={1: 0},
        compiler_params=pltpu.CompilerParams(vmem_limit_bytes=KERNEL_VMEM),
        name="store_last",
    )(in_vmem(head), grads)


def chunk_sizes(head_count):
    tail = [2, 1]
    if head_count < sum(tail) + 2:
        return [1] * head_count
    return [1, head_count - sum(tail) - 1] + tail


def replica_sum(value, axis):
    count = lax.axis_size(axis)
    if count & (count - 1):
        return lax.psum(value, axis)
    stride = 1
    while stride < count:
        value = value + lax.ppermute(value, axis, [(i, i ^ stride) for i in range(count)])
        stride *= 2
    return value


def body(stash, grad_out, doc_lengths):
    by_head = jnp.transpose(stash[0, 0], (1, 0, 2))
    head_count = by_head.shape[0]
    section_count = lax.axis_size("section")
    mirror = [(i, section_count - 1 - i) for i in range(section_count)]
    row_count = by_head.shape[1]
    split = (row_count - 1) // TILE * TILE
    last = head_count - 1
    sizes = chunk_sizes(last)
    firsts = [sum(sizes[:i]) for i in range(len(sizes))]
    pieces = [(slice(first, first + size), slice(None)) for first, size in zip(firsts, sizes)]
    pieces += [(slice(last, None), slice(0, split)), (slice(last, None), slice(split, None))]
    grad_rows, lengths = grad_out[0, 0], doc_lengths[0, 0]
    arrived = []
    for piece in pieces:
        packed, by_head = lax.optimization_barrier((by_head[piece], by_head))
        arrived.append(lax.ppermute(packed, "section", mirror))
    grads, start_row, bias_parts = None, None, []
    for first, packed in zip(firsts, arrived):
        grads, bias, start_row = chunk_grads(
            packed, grad_rows, lengths, head_count, first, start_row, grads
        )
        bias_parts.append(bias)
    early, late = arrived[-2:]
    started = early_grads(early, grad_rows, start_row, last, bias_parts[-1])
    final, bias_own = late_grads(early, late, grad_rows, start_row, started, bias_parts)
    bias_total = replica_sum(bias_own, "dp")
    grads = store_last(final, grads)
    bias_grad = jnp.transpose(bias_total / lax.axis_size("dp"), (1, 0, 2))
    return (jnp.transpose(grads, (1, 0, 2))[None, None], bias_grad)


def solution(mesh):
    in_specs = (
        P("section", "dp", None, "tp", None),
        P("section", "dp", None, "tp"),
        P("section", "dp", None),
    )
    out_specs = (P("section", "dp", None, "tp", None), P("section", "tp", None))
    return jax.shard_map(body, mesh=mesh, in_specs=in_specs, out_specs=out_specs, check_vma=False)
```

```python
import functools
import math

import jax
import jax.numpy as jnp
from jax import lax
from jax.experimental import pallas as pl
from jax.experimental.pallas import tpu as pltpu
from jax.sharding import PartitionSpec as P

MASKED = -1e30
TILE = 128
ROW_TILE = 16
KERNEL_VMEM = 16 * 1024 * 1024


def doc_starts(lengths_ref, row_count):
    query_at = lax.broadcasted_iota(jnp.int32, (1, row_count), 1)
    doc_start = jnp.zeros((1, row_count), jnp.int32)
    doc_end = jnp.int32(0)
    for doc in range(lengths_ref.shape[0]):
        doc_end = doc_end + lengths_ref[doc]
        doc_start = jnp.where(query_at >= doc_end, doc_end, doc_start)
    return doc_start


ROWS_BY_ROWS = (((1,), (1,)), ((), ()))
PLAIN = (((1,), (0,)), ((), ()))
COLUMNS = (((0,), (0,)), ((), ()))
dot = functools.partial(lax.dot_general, preferred_element_type=jnp.float32)


def split_pack(packed):
    head_size = packed.shape[1] // 3
    return (
        packed[:, :head_size],
        packed[:, head_size : 2 * head_size],
        packed[:, 2 * head_size :],
    )


def mask_rows(doc_start, first_query, first_key, key_count):
    shape = (key_count, doc_start.shape[1])
    query_at = first_query + lax.broadcasted_iota(jnp.int32, (1, shape[1]), 1)
    key_at = first_key + lax.broadcasted_iota(jnp.int32, shape, 0)
    return jnp.where((key_at >= doc_start) & (key_at <= query_at), 0.0, MASKED)


def tile_weights(queries, keys_in, values_in, grad_rows, mask):
    inv_root = 1.0 / math.sqrt(queries.shape[1])
    masked = dot(keys_in, queries, ROWS_BY_ROWS) + mask
    row_top = jnp.max(masked, axis=0, keepdims=True)
    raised = jnp.exp2((masked - row_top) * (inv_root * math.log2(math.e)))
    prob = raised * (1.0 / jnp.sum(raised, axis=0, keepdims=True))
    prob_grad = dot(values_in, grad_rows, ROWS_BY_ROWS)
    row_dot = jnp.sum(prob * prob_grad, axis=0, keepdims=True)
    score_grad = (prob * inv_root) * (prob_grad - row_dot)
    return prob.astype(jnp.bfloat16), score_grad.astype(jnp.bfloat16)


def head_grads(packed, grad_rows, doc_start):
    queries, keys_in, values_in = split_pack(packed)
    mask = mask_rows(doc_start, 0, 0, packed.shape[0])
    prob_low, score_low = tile_weights(queries, keys_in, values_in, grad_rows, mask)
    return (
        dot(score_low, keys_in, COLUMNS),
        dot(score_low, queries, PLAIN),
        dot(prob_low, grad_rows, PLAIN),
    )


def write_head(grads, out_ref, out_head, bias_ref, bias_head):
    for part, grad in enumerate(grads):
        head_size = grad.shape[1]
        span = slice(part * head_size, (part + 1) * head_size)
        out_ref[out_head, :, span] = grad.astype(jnp.bfloat16)
        bias_ref[bias_head, :, span] = jnp.sum(grad, axis=0, keepdims=True)


def chunk_kernel(packed_ref, grad_ref, start_ref, _, out_ref, bias_ref, *, first_head):
    head_size = packed_ref.shape[2] // 3
    head = pl.program_id(0)
    grad_at = pl.multiple_of((first_head + head) * head_size, head_size)
    grads = head_grads(packed_ref[head], grad_ref[:, pl.ds(grad_at, head_size)], start_ref[...])
    write_head(grads, out_ref, 0, bias_ref, head)


def first_kernel(lengths_ref, first_ref, rest_ref, grad_ref, out_ref, bias_ref, start_ref):
    head = pl.program_id(0)
    first_count = first_ref.shape[0]
    head_size = first_ref.shape[2] // 3

    @pl.when(head == 0)
    def _():
        start_ref[...] = doc_starts(lengths_ref, first_ref.shape[1])

    packed = jnp.where(
        head < first_count,
        first_ref[jnp.minimum(head, first_count - 1)],
        rest_ref[jnp.maximum(head - first_count, 0)],
    )
    grad_at = pl.multiple_of(head * head_size, head_size)
    grads = head_grads(packed, grad_ref[:, pl.ds(grad_at, head_size)], start_ref[...])
    write_head(grads, out_ref, 0, bias_ref, head)


def column_sum(rows):
    return jnp.sum(rows, axis=0, keepdims=True)


def early_kernel(early_ref, grad_ref, start_ref, _, query_ref, sums_ref, bias_ref, mask_ref, *, head):
    row_count, pack_width = early_ref.shape[1:]
    head_size = pack_width // 3
    queries, keys_in, values_in = split_pack(early_ref[0])
    grad_rows = grad_ref[:row_count, head * head_size : (head + 1) * head_size]
    doc_start = start_ref[...]
    tiles = [slice(at, min(at + TILE, row_count)) for at in range(0, row_count, TILE)]
    key_grads, value_grads = [0.0] * len(tiles), [0.0] * len(tiles)
    query_bias = jnp.zeros((1, head_size), jnp.float32)
    for index, tile in enumerate(tiles):
        seen = slice(0, tile.stop)
        mask = mask_rows(doc_start[:, tile], tile.start, 0, tile.stop)
        prob_low, score_low = tile_weights(
            queries[tile], keys_in[seen], values_in[seen], grad_rows[tile], mask
        )
        query_grad = dot(score_low, keys_in[seen], COLUMNS)
        query_ref[tile] = query_grad.astype(jnp.bfloat16)
        query_bias += column_sum(query_grad)
        for past in range(index + 1):
            key_grads[past] += dot(score_low[tiles[past]], queries[tile], PLAIN)
            value_grads[past] += dot(prob_low[tiles[past]], grad_rows[tile], PLAIN)
    bias_ref[:, :head_size] = query_bias
    for part, grads in enumerate((key_grads, value_grads)):
        for tile, grad in zip(tiles, grads):
            sums_ref[tile, part * head_size : (part + 1) * head_size] = grad
        bias_ref[:, (part + 1) * head_size : (part + 2) * head_size] = sum(map(column_sum, grads))
    first_key = doc_start.shape[1] - mask_ref.shape[0]
    mask_ref[...] = mask_rows(doc_start[:, row_count:], row_count, first_key, mask_ref.shape[0])


def late_kernel(early_ref, late_ref, grad_ref, mask_ref, early_bias_ref, *refs):
    bias_parts, (query_ref, added_ref, bias_ref) = refs[:-3], refs[-3:]
    split = early_ref.shape[1]
    first_key = split + late_ref.shape[1] - mask_ref.shape[0]
    head_size = early_ref.shape[2] // 3
    head = sum(part_ref.shape[0] for part_ref in bias_parts)
    queries = late_ref[0, :, :head_size]
    grad_rows = grad_ref[split:, head * head_size : (head + 1) * head_size]
    keys_in, values_in = (
        jnp.concatenate([early_ref[0, first_key:, span], late_ref[0, :, span]], axis=0)
        for span in (slice(head_size, 2 * head_size), slice(2 * head_size, None))
    )
    prob_low, score_low = tile_weights(queries, keys_in, values_in, grad_rows, mask_ref[...])
    query_grad = dot(score_low, keys_in, COLUMNS)
    key_grad = dot(score_low, queries, PLAIN)
    value_grad = dot(prob_low, grad_rows, PLAIN)
    for part, grad in enumerate((query_grad, key_grad, value_grad)):
        span = slice(part * head_size, (part + 1) * head_size)
        bias_ref[head, :, span] = early_bias_ref[:, span] + column_sum(grad)
    query_ref[...] = query_grad.astype(jnp.bfloat16)
    added_ref[:, :head_size] = key_grad
    added_ref[:, head_size:] = value_grad
    head_at = 0
    for part_ref in bias_parts:
        bias_ref[head_at : head_at + part_ref.shape[0]] = part_ref[...]
        head_at += part_ref.shape[0]


def store_kernel(early_query_ref, sums_ref, late_query_ref, added_ref, _, out_ref, head_ref, semaphore):
    split, head_size = early_query_ref.shape
    first_key = head_ref.shape[1] - added_ref.shape[0]
    head_ref[0, :split, :head_size] = early_query_ref[...]
    head_ref[0, split:, :head_size] = late_query_ref[...]
    head_ref[0, :first_key, head_size:] = sums_ref[:first_key].astype(jnp.bfloat16)
    seen = split - first_key
    head_ref[0, first_key:split, head_size:] = (sums_ref[first_key:] + added_ref[:seen]).astype(
        jnp.bfloat16
    )
    head_ref[0, split:, head_size:] = added_ref[seen:].astype(jnp.bfloat16)
    at = out_ref.shape[0] - 1
    copy = pltpu.make_async_copy(head_ref, out_ref.at[pl.ds(at, 1)], semaphore)
    copy.start()
    copy.wait()


def in_vmem(array):
    return pltpu.with_memory_space_constraint(array, pltpu.VMEM)


VMEM_SPEC = pl.BlockSpec(memory_space=pltpu.VMEM)
SMEM_SPEC = pl.BlockSpec(memory_space=pltpu.SMEM)
ANY_SPEC = pl.BlockSpec(memory_space=pl.ANY)


def grads_outs(chunk_heads, head_count, first_head, row_count, pack_width):
    specs = [
        pl.BlockSpec((1, row_count, pack_width), lambda h: (first_head + h, 0, 0)),
        VMEM_SPEC,
    ]
    shapes = [
        jax.ShapeDtypeStruct((head_count, row_count, pack_width), jnp.bfloat16),
        pltpu.VMEM((chunk_heads, 1, pack_width), jnp.float32),
    ]
    return specs, shapes


def first_grads(first, rest, grad_rows, lengths, head_count):
    _, row_count, pack_width = first.shape
    chunk_heads = first.shape[0] + rest.shape[0]
    specs, shapes = grads_outs(chunk_heads, head_count, 0, row_count, pack_width)
    return pl.pallas_call(
        first_kernel,
        grid=(chunk_heads,),
        in_specs=[SMEM_SPEC, VMEM_SPEC, VMEM_SPEC, VMEM_SPEC],
        out_specs=specs + [VMEM_SPEC],
        out_shape=shapes + [pltpu.VMEM((1, row_count), jnp.int32)],
        compiler_params=pltpu.CompilerParams(vmem_limit_bytes=KERNEL_VMEM),
        name="first_grads",
    )(lengths, in_vmem(first), in_vmem(rest), in_vmem(grad_rows))


def chunk_grads(packed, grad_rows, start_row, first_head, previous):
    chunk_heads, row_count, pack_width = packed.shape
    specs, shapes = grads_outs(chunk_heads, previous.shape[0], first_head, row_count, pack_width)
    return pl.pallas_call(
        functools.partial(chunk_kernel, first_head=first_head),
        grid=(chunk_heads,),
        in_specs=[VMEM_SPEC, VMEM_SPEC, VMEM_SPEC, ANY_SPEC],
        out_specs=specs,
        out_shape=shapes,
        input_output_aliases={3: 0},
        compiler_params=pltpu.CompilerParams(vmem_limit_bytes=KERNEL_VMEM),
    )(in_vmem(packed), in_vmem(grad_rows), in_vmem(start_row), previous)


def early_grads(packed, grad_rows, start_row, head, after):
    _, split, pack_width = packed.shape
    row_count, head_size = grad_rows.shape[0], pack_width // 3
    longest = row_count // 2
    first_key = max(0, split + 1 - longest) // ROW_TILE * ROW_TILE
    return pl.pallas_call(
        functools.partial(early_kernel, head=head),
        in_specs=[VMEM_SPEC] * 4,
        out_specs=[VMEM_SPEC] * 4,
        out_shape=[
            pltpu.VMEM((split, head_size), jnp.bfloat16),
            pltpu.VMEM((split, 2 * head_size), jnp.float32),
            pltpu.VMEM((1, pack_width), jnp.float32),
            pltpu.VMEM((row_count - first_key, row_count - split), jnp.float32),
        ],
        compiler_params=pltpu.CompilerParams(vmem_limit_bytes=KERNEL_VMEM),
        name="early_grads",
    )(*map(in_vmem, (packed, grad_rows, start_row, after)))


def late_grads(early, late, grad_rows, mask, early_bias, bias_parts):
    head_count = 1 + sum(part.shape[0] for part in bias_parts)
    pack_width = early.shape[2]
    head_size = pack_width // 3
    operands = [early, late, grad_rows, mask, early_bias, *bias_parts]
    return pl.pallas_call(
        late_kernel,
        in_specs=[VMEM_SPEC] * len(operands),
        out_specs=[VMEM_SPEC] * 3,
        out_shape=[
            pltpu.VMEM((late.shape[1], head_size), jnp.bfloat16),
            pltpu.VMEM((mask.shape[0], 2 * head_size), jnp.float32),
            pltpu.VMEM((head_count, 1, pack_width), jnp.float32),
        ],
        compiler_params=pltpu.CompilerParams(vmem_limit_bytes=KERNEL_VMEM),
        name="late_grads",
    )(*map(in_vmem, operands))


def store_last(parts, grads):
    return pl.pallas_call(
        store_kernel,
        in_specs=[VMEM_SPEC] * len(parts) + [ANY_SPEC],
        out_specs=ANY_SPEC,
        out_shape=jax.ShapeDtypeStruct(grads.shape, grads.dtype),
        scratch_shapes=[pltpu.VMEM((1, *grads.shape[1:]), grads.dtype), pltpu.SemaphoreType.DMA],
        input_output_aliases={len(parts): 0},
        compiler_params=pltpu.CompilerParams(vmem_limit_bytes=KERNEL_VMEM),
        name="store_last",
    )(*map(in_vmem, parts), grads)


def chunk_sizes(head_count):
    tail = min(2, head_count // 2)
    return [1, head_count - 1 - tail, tail]


def replica_sum(value, axis):
    count = lax.axis_size(axis)
    if count & (count - 1):
        return lax.psum(value, axis)
    stride = 1
    while stride < count:
        value = value + lax.ppermute(value, axis, [(i, i ^ stride) for i in range(count)])
        stride *= 2
    return value


def body(stash, grad_out, doc_lengths):
    by_head = jnp.transpose(stash[0, 0], (1, 0, 2))
    head_count = by_head.shape[0]
    section_count = lax.axis_size("section")
    mirror = [(i, section_count - 1 - i) for i in range(section_count)]
    row_count = by_head.shape[1]
    split = row_count - row_count * 3 // 10 // ROW_TILE * ROW_TILE
    last = head_count - 1
    sizes = chunk_sizes(last)
    firsts = [sum(sizes[:i]) for i in range(len(sizes))]
    pieces = [(slice(first, first + size), slice(None)) for first, size in zip(firsts, sizes)]
    pieces += [(slice(last, None), slice(0, split)), (slice(last, None), slice(split, None))]
    grad_rows, lengths = grad_out[0, 0], doc_lengths[0, 0]
    arrived = []
    for piece in pieces:
        packed, by_head = lax.optimization_barrier((by_head[piece], by_head))
        arrived.append(lax.ppermute(packed, "section", mirror))
    grads, bias, start_row = first_grads(*arrived[:2], grad_rows, lengths, head_count)
    bias_parts = [bias]
    for first, packed in zip(firsts[2:], arrived[2:]):
        grads, bias = chunk_grads(packed, grad_rows, start_row, first, grads)
        bias_parts.append(bias)
    early, late = arrived[-2:]
    query_early, sums, early_bias, mask = early_grads(
        early, grad_rows, start_row, last, bias_parts[-1]
    )
    query_late, added, bias_own = late_grads(early, late, grad_rows, mask, early_bias, bias_parts)
    bias_total = replica_sum(bias_own, "dp")
    grads = store_last((query_early, sums, query_late, added), grads)
    bias_grad = jnp.transpose(bias_total / lax.axis_size("dp"), (1, 0, 2))
    return (jnp.transpose(grads, (1, 0, 2))[None, None], bias_grad)


def solution(mesh):
    in_specs = (
        P("section", "dp", None, "tp", None),
        P("section", "dp", None, "tp"),
        P("section", "dp", None),
    )
    out_specs = (P("section", "dp", None, "tp", None), P("section", "tp", None))
    return jax.shard_map(body, mesh=mesh, in_specs=in_specs, out_specs=out_specs, check_vma=False)
```

```python
import functools
import math

import jax
import jax.numpy as jnp
from jax import lax
from jax.experimental import pallas as pl
from jax.experimental.pallas import tpu as pltpu
from jax.sharding import PartitionSpec as P

MASKED = -1e30
TILE = 128
ROW_TILE = 16
KERNEL_VMEM = 16 * 1024 * 1024


def doc_starts(lengths_ref, row_count):
    query_at = lax.broadcasted_iota(jnp.int32, (1, row_count), 1)
    doc_start = jnp.zeros((1, row_count), jnp.int32)
    doc_end = jnp.int32(0)
    for doc in range(lengths_ref.shape[0]):
        doc_end = doc_end + lengths_ref[doc]
        doc_start = jnp.where(query_at >= doc_end, doc_end, doc_start)
    return doc_start


ROWS_BY_ROWS = (((1,), (1,)), ((), ()))
PLAIN = (((1,), (0,)), ((), ()))
COLUMNS = (((0,), (0,)), ((), ()))
dot = functools.partial(lax.dot_general, preferred_element_type=jnp.float32)


def split_pack(packed):
    head_size = packed.shape[1] // 3
    return (
        packed[:, :head_size],
        packed[:, head_size : 2 * head_size],
        packed[:, 2 * head_size :],
    )


def mask_rows(doc_start, first_query, first_key, key_count):
    shape = (key_count, doc_start.shape[1])
    query_at = first_query + lax.broadcasted_iota(jnp.int32, (1, shape[1]), 1)
    key_at = first_key + lax.broadcasted_iota(jnp.int32, shape, 0)
    return jnp.where((key_at >= doc_start) & (key_at <= query_at), 0.0, MASKED)


def tile_weights(queries, keys_in, values_in, grad_rows, mask):
    inv_root = 1.0 / math.sqrt(queries.shape[1])
    masked = dot(keys_in, queries, ROWS_BY_ROWS) + mask
    row_top = jnp.max(masked, axis=0, keepdims=True)
    raised = jnp.exp2((masked - row_top) * (inv_root * math.log2(math.e)))
    prob = raised * (1.0 / jnp.sum(raised, axis=0, keepdims=True))
    prob_grad = dot(values_in, grad_rows, ROWS_BY_ROWS)
    row_dot = jnp.sum(prob * prob_grad, axis=0, keepdims=True)
    score_grad = (prob * inv_root) * (prob_grad - row_dot)
    return prob.astype(jnp.bfloat16), score_grad.astype(jnp.bfloat16)


def head_grads(packed, grad_rows, doc_start):
    queries, keys_in, values_in = split_pack(packed)
    mask = mask_rows(doc_start, 0, 0, packed.shape[0])
    prob_low, score_low = tile_weights(queries, keys_in, values_in, grad_rows, mask)
    return (
        dot(score_low, keys_in, COLUMNS),
        dot(score_low, queries, PLAIN),
        dot(prob_low, grad_rows, PLAIN),
    )


def write_head(grads, out_ref, out_head, bias_ref, bias_head):
    for part, grad in enumerate(grads):
        head_size = grad.shape[1]
        span = slice(part * head_size, (part + 1) * head_size)
        out_ref[out_head, :, span] = grad.astype(jnp.bfloat16)
        bias_ref[bias_head, :, span] = jnp.sum(grad, axis=0, keepdims=True)


def chunk_kernel(packed_ref, grad_ref, start_ref, _, out_ref, bias_ref, *, first_head):
    head_size = packed_ref.shape[2] // 3
    head = pl.program_id(0)
    grad_at = pl.multiple_of((first_head + head) * head_size, head_size)
    grads = head_grads(packed_ref[head], grad_ref[:, pl.ds(grad_at, head_size)], start_ref[...])
    write_head(grads, out_ref, 0, bias_ref, head)


def first_kernel(lengths_ref, first_ref, rest_ref, grad_ref, out_ref, bias_ref, start_ref):
    head = pl.program_id(0)
    first_count = first_ref.shape[0]
    head_size = first_ref.shape[2] // 3

    @pl.when(head == 0)
    def _():
        start_ref[...] = doc_starts(lengths_ref, first_ref.shape[1])

    packed = jnp.where(
        head < first_count,
        first_ref[jnp.minimum(head, first_count - 1)],
        rest_ref[jnp.maximum(head - first_count, 0)],
    )
    grad_at = pl.multiple_of(head * head_size, head_size)
    grads = head_grads(packed, grad_ref[:, pl.ds(grad_at, head_size)], start_ref[...])
    write_head(grads, out_ref, 0, bias_ref, head)


def column_sum(rows):
    return jnp.sum(rows, axis=0, keepdims=True)


def early_kernel(early_ref, grad_ref, start_ref, _, query_ref, sums_ref, bias_ref, mask_ref, *, head):
    row_count, pack_width = early_ref.shape[1:]
    head_size = pack_width // 3
    queries, keys_in, values_in = split_pack(early_ref[0])
    grad_rows = grad_ref[:row_count, head * head_size : (head + 1) * head_size]
    doc_start = start_ref[...]
    tiles = [slice(at, min(at + TILE, row_count)) for at in range(0, row_count, TILE)]
    key_grads, value_grads = [0.0] * len(tiles), [0.0] * len(tiles)
    query_bias = jnp.zeros((1, head_size), jnp.float32)
    for index, tile in enumerate(tiles):
        seen = slice(0, tile.stop)
        mask = mask_rows(doc_start[:, tile], tile.start, 0, tile.stop)
        prob_low, score_low = tile_weights(
            queries[tile], keys_in[seen], values_in[seen], grad_rows[tile], mask
        )
        query_grad = dot(score_low, keys_in[seen], COLUMNS)
        query_ref[tile] = query_grad.astype(jnp.bfloat16)
        query_bias += column_sum(query_grad)
        for past in range(index + 1):
            key_grads[past] += dot(score_low[tiles[past]], queries[tile], PLAIN)
            value_grads[past] += dot(prob_low[tiles[past]], grad_rows[tile], PLAIN)
    bias_ref[:, :head_size] = query_bias
    for part, grads in enumerate((key_grads, value_grads)):
        for tile, grad in zip(tiles, grads):
            sums_ref[tile, part * head_size : (part + 1) * head_size] = grad
        bias_ref[:, (part + 1) * head_size : (part + 2) * head_size] = sum(map(column_sum, grads))
    first_key = doc_start.shape[1] - mask_ref.shape[0]
    mask_ref[...] = mask_rows(doc_start[:, row_count:], row_count, first_key, mask_ref.shape[0])


def late_kernel(early_ref, late_ref, grad_ref, mask_ref, early_bias_ref, *refs):
    bias_parts, (query_ref, added_ref, bias_ref) = refs[:-3], refs[-3:]
    split = early_ref.shape[1]
    first_key = split + late_ref.shape[1] - mask_ref.shape[0]
    head_size = early_ref.shape[2] // 3
    head = sum(part_ref.shape[0] for part_ref in bias_parts)
    queries = late_ref[0, :, :head_size]
    grad_rows = grad_ref[split:, head * head_size : (head + 1) * head_size]
    keys_in, values_in = (
        jnp.concatenate([early_ref[0, first_key:, span], late_ref[0, :, span]], axis=0)
        for span in (slice(head_size, 2 * head_size), slice(2 * head_size, None))
    )
    prob_low, score_low = tile_weights(queries, keys_in, values_in, grad_rows, mask_ref[...])
    query_grad = dot(score_low, keys_in, COLUMNS)
    key_grad = dot(score_low, queries, PLAIN)
    value_grad = dot(prob_low, grad_rows, PLAIN)
    for part, grad in enumerate((query_grad, key_grad, value_grad)):
        span = slice(part * head_size, (part + 1) * head_size)
        bias_ref[head, :, span] = early_bias_ref[:, span] + column_sum(grad)
    query_ref[...] = query_grad.astype(jnp.bfloat16)
    added_ref[:, :head_size] = key_grad
    added_ref[:, head_size:] = value_grad
    head_at = 0
    for part_ref in bias_parts:
        bias_ref[head_at : head_at + part_ref.shape[0]] = part_ref[...]
        head_at += part_ref.shape[0]


def store_kernel(early_query_ref, sums_ref, late_query_ref, added_ref, _, out_ref, head_ref, semaphore):
    split, head_size = early_query_ref.shape
    first_key = head_ref.shape[1] - added_ref.shape[0]
    head_ref[0, :split, :head_size] = early_query_ref[...]
    head_ref[0, split:, :head_size] = late_query_ref[...]
    head_ref[0, :first_key, head_size:] = sums_ref[:first_key].astype(jnp.bfloat16)
    seen = split - first_key
    head_ref[0, first_key:split, head_size:] = (sums_ref[first_key:] + added_ref[:seen]).astype(
        jnp.bfloat16
    )
    head_ref[0, split:, head_size:] = added_ref[seen:].astype(jnp.bfloat16)
    at = out_ref.shape[0] - 1
    copy = pltpu.make_async_copy(head_ref, out_ref.at[pl.ds(at, 1)], semaphore)
    copy.start()
    copy.wait()


def in_vmem(array):
    return pltpu.with_memory_space_constraint(array, pltpu.VMEM)


VMEM_SPEC = pl.BlockSpec(memory_space=pltpu.VMEM)
SMEM_SPEC = pl.BlockSpec(memory_space=pltpu.SMEM)
ANY_SPEC = pl.BlockSpec(memory_space=pl.ANY)


def grads_outs(chunk_heads, head_count, first_head, row_count, pack_width):
    specs = [
        pl.BlockSpec((1, row_count, pack_width), lambda h: (first_head + h, 0, 0)),
        VMEM_SPEC,
    ]
    shapes = [
        jax.ShapeDtypeStruct((head_count, row_count, pack_width), jnp.bfloat16),
        pltpu.VMEM((chunk_heads, 1, pack_width), jnp.float32),
    ]
    return specs, shapes


def first_grads(first, rest, grad_rows, lengths, head_count):
    _, row_count, pack_width = first.shape
    chunk_heads = first.shape[0] + rest.shape[0]
    specs, shapes = grads_outs(chunk_heads, head_count, 0, row_count, pack_width)
    return pl.pallas_call(
        first_kernel,
        grid=(chunk_heads,),
        in_specs=[SMEM_SPEC, VMEM_SPEC, VMEM_SPEC, VMEM_SPEC],
        out_specs=specs + [VMEM_SPEC],
        out_shape=shapes + [pltpu.VMEM((1, row_count), jnp.int32)],
        compiler_params=pltpu.CompilerParams(vmem_limit_bytes=KERNEL_VMEM),
        name="first_grads",
    )(lengths, in_vmem(first), in_vmem(rest), in_vmem(grad_rows))


def chunk_grads(packed, grad_rows, start_row, first_head, previous):
    chunk_heads, row_count, pack_width = packed.shape
    specs, shapes = grads_outs(chunk_heads, previous.shape[0], first_head, row_count, pack_width)
    return pl.pallas_call(
        functools.partial(chunk_kernel, first_head=first_head),
        grid=(chunk_heads,),
        in_specs=[VMEM_SPEC, VMEM_SPEC, VMEM_SPEC, ANY_SPEC],
        out_specs=specs,
        out_shape=shapes,
        input_output_aliases={3: 0},
        compiler_params=pltpu.CompilerParams(vmem_limit_bytes=KERNEL_VMEM),
    )(in_vmem(packed), in_vmem(grad_rows), in_vmem(start_row), previous)


def early_grads(packed, grad_rows, start_row, head, after):
    _, split, pack_width = packed.shape
    row_count, head_size = grad_rows.shape[0], pack_width // 3
    longest = row_count // 2
    first_key = max(0, split + 1 - longest) // ROW_TILE * ROW_TILE
    return pl.pallas_call(
        functools.partial(early_kernel, head=head),
        in_specs=[VMEM_SPEC] * 4,
        out_specs=[VMEM_SPEC] * 4,
        out_shape=[
            pltpu.VMEM((split, head_size), jnp.bfloat16),
            pltpu.VMEM((split, 2 * head_size), jnp.float32),
            pltpu.VMEM((1, pack_width), jnp.float32),
            pltpu.VMEM((row_count - first_key, row_count - split), jnp.float32),
        ],
        compiler_params=pltpu.CompilerParams(vmem_limit_bytes=KERNEL_VMEM),
        name="early_grads",
    )(*map(in_vmem, (packed, grad_rows, start_row, after)))


def late_grads(early, late, grad_rows, mask, early_bias, bias_parts):
    head_count = 1 + sum(part.shape[0] for part in bias_parts)
    pack_width = early.shape[2]
    head_size = pack_width // 3
    operands = [early, late, grad_rows, mask, early_bias, *bias_parts]
    return pl.pallas_call(
        late_kernel,
        in_specs=[VMEM_SPEC] * len(operands),
        out_specs=[VMEM_SPEC] * 3,
        out_shape=[
            pltpu.VMEM((late.shape[1], head_size), jnp.bfloat16),
            pltpu.VMEM((mask.shape[0], 2 * head_size), jnp.float32),
            pltpu.VMEM((head_count, 1, pack_width), jnp.float32),
        ],
        compiler_params=pltpu.CompilerParams(vmem_limit_bytes=KERNEL_VMEM),
        name="late_grads",
    )(*map(in_vmem, operands))


def store_last(parts, grads):
    return pl.pallas_call(
        store_kernel,
        in_specs=[VMEM_SPEC] * len(parts) + [ANY_SPEC],
        out_specs=ANY_SPEC,
        out_shape=jax.ShapeDtypeStruct(grads.shape, grads.dtype),
        scratch_shapes=[pltpu.VMEM((1, *grads.shape[1:]), grads.dtype), pltpu.SemaphoreType.DMA],
        input_output_aliases={len(parts): 0},
        compiler_params=pltpu.CompilerParams(vmem_limit_bytes=KERNEL_VMEM),
        name="store_last",
    )(*map(in_vmem, parts), grads)


def cut_kernel(source_ref, *refs, at):
    out_ref, semaphore = refs[-2:]
    window = tuple(pl.ds(start, size) for start, size in zip(at, out_ref.shape))
    copy = pltpu.make_async_copy(source_ref.at[window], out_ref, semaphore)
    copy.start()
    copy.wait()


def cut(source, at, shape, after):
    operands = [pltpu.with_memory_space_constraint(source, pltpu.HBM)]
    in_specs = [pl.BlockSpec(memory_space=pltpu.HBM)]
    if after is not None:
        operands.append(after)
        in_specs.append(ANY_SPEC)
    return pl.pallas_call(
        functools.partial(cut_kernel, at=at),
        in_specs=in_specs,
        out_specs=VMEM_SPEC,
        out_shape=pltpu.VMEM(shape, source.dtype),
        scratch_shapes=[pltpu.SemaphoreType.DMA],
        compiler_params=pltpu.CompilerParams(vmem_limit_bytes=KERNEL_VMEM),
        name="cut",
    )(*operands)


def chunk_sizes(head_count):
    tail = min(2, head_count // 2)
    return [1, head_count - 1 - tail, tail]


def replica_sum(value, axis):
    count = lax.axis_size(axis)
    if count & (count - 1):
        return lax.psum(value, axis)
    stride = 1
    while stride < count:
        value = value + lax.ppermute(value, axis, [(i, i ^ stride) for i in range(count)])
        stride *= 2
    return value


def body(stash, grad_out, doc_lengths):
    by_head = jnp.transpose(stash[0, 0], (1, 0, 2))
    head_count = by_head.shape[0]
    section_count = lax.axis_size("section")
    mirror = [(i, section_count - 1 - i) for i in range(section_count)]
    row_count = by_head.shape[1]
    split = row_count - row_count * 3 // 10 // ROW_TILE * ROW_TILE
    last = head_count - 1
    sizes = chunk_sizes(last)
    firsts = [sum(sizes[:i]) for i in range(len(sizes))]
    pieces = [(first, size, 0, row_count) for first, size in zip(firsts, sizes)]
    pieces += [(last, 1, 0, split), (last, 1, split, row_count - split)]
    grad_rows, lengths = grad_out[0, 0], doc_lengths[0, 0]
    arrived = []
    packed = None
    for head, heads, row, rows in pieces:
        packed = cut(by_head, (head, row, 0), (heads, rows, by_head.shape[2]), packed)
        arrived.append(lax.ppermute(packed, "section", mirror))
    grad_rows = cut(grad_rows, (0, 0), grad_rows.shape, packed)
    grads, bias, start_row = first_grads(*arrived[:2], grad_rows, lengths, head_count)
    bias_parts = [bias]
    for first, packed in zip(firsts[2:], arrived[2:]):
        grads, bias = chunk_grads(packed, grad_rows, start_row, first, grads)
        bias_parts.append(bias)
    early, late = arrived[-2:]
    query_early, sums, early_bias, mask = early_grads(
        early, grad_rows, start_row, last, bias_parts[-1]
    )
    query_late, added, bias_own = late_grads(early, late, grad_rows, mask, early_bias, bias_parts)
    bias_total = replica_sum(bias_own, "dp")
    grads = store_last((query_early, sums, query_late, added), grads)
    bias_grad = jnp.transpose(bias_total / lax.axis_size("dp"), (1, 0, 2))
    return (jnp.transpose(grads, (1, 0, 2))[None, None], bias_grad)


def solution(mesh):
    in_specs = (
        P("section", "dp", None, "tp", None),
        P("section", "dp", None, "tp"),
        P("section", "dp", None),
    )
    out_specs = (P("section", "dp", None, "tp", None), P("section", "tp", None))
    return jax.shard_map(body, mesh=mesh, in_specs=in_specs, out_specs=out_specs, check_vma=False)
```

```python
import functools
import math

import jax
import jax.numpy as jnp
from jax import lax
from jax.experimental import pallas as pl
from jax.experimental.pallas import tpu as pltpu
from jax.sharding import PartitionSpec as P

MASKED = -1e30
TILE = 128
ROW_TILE = 16
KERNEL_VMEM = 16 * 1024 * 1024


def doc_starts(lengths_ref, row_count):
    query_at = lax.broadcasted_iota(jnp.int32, (1, row_count), 1)
    doc_start = jnp.zeros((1, row_count), jnp.int32)
    doc_end = jnp.int32(0)
    for doc in range(lengths_ref.shape[0]):
        doc_end = doc_end + lengths_ref[doc]
        doc_start = jnp.where(query_at >= doc_end, doc_end, doc_start)
    return doc_start


ROWS_BY_ROWS = (((1,), (1,)), ((), ()))
PLAIN = (((1,), (0,)), ((), ()))
COLUMNS = (((0,), (0,)), ((), ()))
dot = functools.partial(lax.dot_general, preferred_element_type=jnp.float32)


def split_pack(packed):
    head_size = packed.shape[1] // 3
    return (
        packed[:, :head_size],
        packed[:, head_size : 2 * head_size],
        packed[:, 2 * head_size :],
    )


def mask_rows(doc_start, first_query, first_key, key_count):
    shape = (key_count, doc_start.shape[1])
    query_at = first_query + lax.broadcasted_iota(jnp.int32, (1, shape[1]), 1)
    key_at = first_key + lax.broadcasted_iota(jnp.int32, shape, 0)
    return jnp.where((key_at >= doc_start) & (key_at <= query_at), 0.0, MASKED)


def tile_weights(queries, keys_in, values_in, grad_rows, mask):
    inv_root = 1.0 / math.sqrt(queries.shape[1])
    masked = dot(keys_in, queries, ROWS_BY_ROWS) + mask
    row_top = jnp.max(masked, axis=0, keepdims=True)
    raised = jnp.exp2((masked - row_top) * (inv_root * math.log2(math.e)))
    prob = raised * (1.0 / jnp.sum(raised, axis=0, keepdims=True))
    prob_low = prob.astype(jnp.bfloat16)
    prob_grad = dot(values_in, grad_rows, ROWS_BY_ROWS)
    row_dot = jnp.sum(prob_low.astype(jnp.float32) * prob_grad, axis=0, keepdims=True)
    score_grad = (prob * inv_root) * (prob_grad - row_dot)
    return prob_low, score_grad.astype(jnp.bfloat16)


def head_grads(packed, grad_rows, doc_start):
    queries, keys_in, values_in = split_pack(packed)
    mask = mask_rows(doc_start, 0, 0, packed.shape[0])
    prob_low, score_low = tile_weights(queries, keys_in, values_in, grad_rows, mask)
    return (
        dot(score_low, keys_in, COLUMNS),
        dot(score_low, queries, PLAIN),
        dot(prob_low, grad_rows, PLAIN),
    )


def write_head(grads, out_ref, out_head, bias_ref, bias_head):
    for part, grad in enumerate(grads):
        head_size = grad.shape[1]
        span = slice(part * head_size, (part + 1) * head_size)
        out_ref[out_head, :, span] = grad.astype(jnp.bfloat16)
        bias_ref[bias_head, :, span] = jnp.sum(grad, axis=0, keepdims=True)


def chunk_kernel(packed_ref, grad_ref, start_ref, _, out_ref, bias_ref, *, first_head):
    head_size = packed_ref.shape[2] // 3
    head = pl.program_id(0)
    grad_at = pl.multiple_of((first_head + head) * head_size, head_size)
    grads = head_grads(packed_ref[head], grad_ref[:, pl.ds(grad_at, head_size)], start_ref[...])
    write_head(grads, out_ref, 0, bias_ref, head)


def first_kernel(lengths_ref, first_ref, rest_ref, grad_ref, out_ref, bias_ref, start_ref):
    head = pl.program_id(0)
    first_count = first_ref.shape[0]
    head_size = first_ref.shape[2] // 3

    @pl.when(head == 0)
    def _():
        start_ref[...] = doc_starts(lengths_ref, first_ref.shape[1])

    packed = jnp.where(
        head < first_count,
        first_ref[jnp.minimum(head, first_count - 1)],
        rest_ref[jnp.maximum(head - first_count, 0)],
    )
    grad_at = pl.multiple_of(head * head_size, head_size)
    grads = head_grads(packed, grad_ref[:, pl.ds(grad_at, head_size)], start_ref[...])
    write_head(grads, out_ref, 0, bias_ref, head)


def column_sum(rows):
    return jnp.sum(rows, axis=0, keepdims=True)


def early_kernel(early_ref, grad_ref, start_ref, _, query_ref, sums_ref, bias_ref, mask_ref, *, head):
    row_count, pack_width = early_ref.shape[1:]
    head_size = pack_width // 3
    queries, keys_in, values_in = split_pack(early_ref[0])
    grad_rows = grad_ref[:row_count, head * head_size : (head + 1) * head_size]
    doc_start = start_ref[...]
    tiles = [slice(at, min(at + TILE, row_count)) for at in range(0, row_count, TILE)]
    key_grads, value_grads = [0.0] * len(tiles), [0.0] * len(tiles)
    query_bias = jnp.zeros((1, head_size), jnp.float32)
    for index, tile in enumerate(tiles):
        seen = slice(0, tile.stop)
        mask = mask_rows(doc_start[:, tile], tile.start, 0, tile.stop)
        prob_low, score_low = tile_weights(
            queries[tile], keys_in[seen], values_in[seen], grad_rows[tile], mask
        )
        query_grad = dot(score_low, keys_in[seen], COLUMNS)
        query_ref[tile] = query_grad.astype(jnp.bfloat16)
        query_bias += column_sum(query_grad)
        for past in range(index + 1):
            key_grads[past] += dot(score_low[tiles[past]], queries[tile], PLAIN)
            value_grads[past] += dot(prob_low[tiles[past]], grad_rows[tile], PLAIN)
    bias_ref[:, :head_size] = query_bias
    for part, grads in enumerate((key_grads, value_grads)):
        for tile, grad in zip(tiles, grads):
            sums_ref[tile, part * head_size : (part + 1) * head_size] = grad
        bias_ref[:, (part + 1) * head_size : (part + 2) * head_size] = sum(map(column_sum, grads))
    first_key = doc_start.shape[1] - mask_ref.shape[0]
    mask_ref[...] = mask_rows(doc_start[:, row_count:], row_count, first_key, mask_ref.shape[0])


def late_kernel(early_ref, late_ref, grad_ref, mask_ref, early_bias_ref, *refs):
    bias_parts, (query_ref, added_ref, bias_ref) = refs[:-3], refs[-3:]
    split = early_ref.shape[1]
    first_key = split + late_ref.shape[1] - mask_ref.shape[0]
    head_size = early_ref.shape[2] // 3
    head = sum(part_ref.shape[0] for part_ref in bias_parts)
    queries = late_ref[0, :, :head_size]
    grad_rows = grad_ref[split:, head * head_size : (head + 1) * head_size]
    keys_in, values_in = (
        jnp.concatenate([early_ref[0, first_key:, span], late_ref[0, :, span]], axis=0)
        for span in (slice(head_size, 2 * head_size), slice(2 * head_size, None))
    )
    prob_low, score_low = tile_weights(queries, keys_in, values_in, grad_rows, mask_ref[...])
    query_grad = dot(score_low, keys_in, COLUMNS)
    key_grad = dot(score_low, queries, PLAIN)
    value_grad = dot(prob_low, grad_rows, PLAIN)
    for part, grad in enumerate((query_grad, key_grad, value_grad)):
        span = slice(part * head_size, (part + 1) * head_size)
        bias_ref[head, :, span] = early_bias_ref[:, span] + column_sum(grad)
    query_ref[...] = query_grad.astype(jnp.bfloat16)
    added_ref[:, :head_size] = key_grad
    added_ref[:, head_size:] = value_grad
    head_at = 0
    for part_ref in bias_parts:
        bias_ref[head_at : head_at + part_ref.shape[0]] = part_ref[...]
        head_at += part_ref.shape[0]


def store_kernel(early_query_ref, sums_ref, late_query_ref, added_ref, _, out_ref, head_ref, semaphore):
    split, head_size = early_query_ref.shape
    first_key = head_ref.shape[1] - added_ref.shape[0]
    head_ref[0, :split, :head_size] = early_query_ref[...]
    head_ref[0, split:, :head_size] = late_query_ref[...]
    head_ref[0, :first_key, head_size:] = sums_ref[:first_key].astype(jnp.bfloat16)
    seen = split - first_key
    head_ref[0, first_key:split, head_size:] = (sums_ref[first_key:] + added_ref[:seen]).astype(
        jnp.bfloat16
    )
    head_ref[0, split:, head_size:] = added_ref[seen:].astype(jnp.bfloat16)
    at = out_ref.shape[0] - 1
    copy = pltpu.make_async_copy(head_ref, out_ref.at[pl.ds(at, 1)], semaphore)
    copy.start()
    copy.wait()


def in_vmem(array):
    return pltpu.with_memory_space_constraint(array, pltpu.VMEM)


VMEM_SPEC = pl.BlockSpec(memory_space=pltpu.VMEM)
SMEM_SPEC = pl.BlockSpec(memory_space=pltpu.SMEM)
ANY_SPEC = pl.BlockSpec(memory_space=pl.ANY)


def grads_outs(chunk_heads, head_count, first_head, row_count, pack_width):
    specs = [
        pl.BlockSpec((1, row_count, pack_width), lambda h: (first_head + h, 0, 0)),
        VMEM_SPEC,
    ]
    shapes = [
        jax.ShapeDtypeStruct((head_count, row_count, pack_width), jnp.bfloat16),
        pltpu.VMEM((chunk_heads, 1, pack_width), jnp.float32),
    ]
    return specs, shapes


def first_grads(first, rest, grad_rows, lengths, head_count):
    _, row_count, pack_width = first.shape
    chunk_heads = first.shape[0] + rest.shape[0]
    specs, shapes = grads_outs(chunk_heads, head_count, 0, row_count, pack_width)
    return pl.pallas_call(
        first_kernel,
        grid=(chunk_heads,),
        in_specs=[SMEM_SPEC, VMEM_SPEC, VMEM_SPEC, VMEM_SPEC],
        out_specs=specs + [VMEM_SPEC],
        out_shape=shapes + [pltpu.VMEM((1, row_count), jnp.int32)],
        compiler_params=pltpu.CompilerParams(vmem_limit_bytes=KERNEL_VMEM),
        name="first_grads",
    )(lengths, in_vmem(first), in_vmem(rest), in_vmem(grad_rows))


def chunk_grads(packed, grad_rows, start_row, first_head, previous):
    chunk_heads, row_count, pack_width = packed.shape
    specs, shapes = grads_outs(chunk_heads, previous.shape[0], first_head, row_count, pack_width)
    return pl.pallas_call(
        functools.partial(chunk_kernel, first_head=first_head),
        grid=(chunk_heads,),
        in_specs=[VMEM_SPEC, VMEM_SPEC, VMEM_SPEC, ANY_SPEC],
        out_specs=specs,
        out_shape=shapes,
        input_output_aliases={3: 0},
        compiler_params=pltpu.CompilerParams(vmem_limit_bytes=KERNEL_VMEM),
    )(in_vmem(packed), in_vmem(grad_rows), in_vmem(start_row), previous)


def early_grads(packed, grad_rows, start_row, head, after):
    _, split, pack_width = packed.shape
    row_count, head_size = grad_rows.shape[0], pack_width // 3
    longest = row_count // 2
    first_key = max(0, split + 1 - longest) // ROW_TILE * ROW_TILE
    return pl.pallas_call(
        functools.partial(early_kernel, head=head),
        in_specs=[VMEM_SPEC] * 4,
        out_specs=[VMEM_SPEC] * 4,
        out_shape=[
            pltpu.VMEM((split, head_size), jnp.bfloat16),
            pltpu.VMEM((split, 2 * head_size), jnp.float32),
            pltpu.VMEM((1, pack_width), jnp.float32),
            pltpu.VMEM((row_count - first_key, row_count - split), jnp.float32),
        ],
        compiler_params=pltpu.CompilerParams(vmem_limit_bytes=KERNEL_VMEM),
        name="early_grads",
    )(*map(in_vmem, (packed, grad_rows, start_row, after)))


def late_grads(early, late, grad_rows, mask, early_bias, bias_parts):
    head_count = 1 + sum(part.shape[0] for part in bias_parts)
    pack_width = early.shape[2]
    head_size = pack_width // 3
    operands = [early, late, grad_rows, mask, early_bias, *bias_parts]
    return pl.pallas_call(
        late_kernel,
        in_specs=[VMEM_SPEC] * len(operands),
        out_specs=[VMEM_SPEC] * 3,
        out_shape=[
            pltpu.VMEM((late.shape[1], head_size), jnp.bfloat16),
            pltpu.VMEM((mask.shape[0], 2 * head_size), jnp.float32),
            pltpu.VMEM((head_count, 1, pack_width), jnp.float32),
        ],
        compiler_params=pltpu.CompilerParams(vmem_limit_bytes=KERNEL_VMEM),
        name="late_grads",
    )(*map(in_vmem, operands))


def store_last(parts, grads):
    return pl.pallas_call(
        store_kernel,
        in_specs=[VMEM_SPEC] * len(parts) + [ANY_SPEC],
        out_specs=ANY_SPEC,
        out_shape=jax.ShapeDtypeStruct(grads.shape, grads.dtype),
        scratch_shapes=[pltpu.VMEM((1, *grads.shape[1:]), grads.dtype), pltpu.SemaphoreType.DMA],
        input_output_aliases={len(parts): 0},
        compiler_params=pltpu.CompilerParams(vmem_limit_bytes=KERNEL_VMEM),
        name="store_last",
    )(*map(in_vmem, parts), grads)


def cut_kernel(source_ref, *refs, at):
    out_ref, semaphore = refs[-2:]
    window = tuple(pl.ds(start, size) for start, size in zip(at, out_ref.shape))
    copy = pltpu.make_async_copy(source_ref.at[window], out_ref, semaphore)
    copy.start()
    copy.wait()


def cut(source, at, shape, after):
    operands = [pltpu.with_memory_space_constraint(source, pltpu.HBM)]
    in_specs = [pl.BlockSpec(memory_space=pltpu.HBM)]
    if after is not None:
        operands.append(after)
        in_specs.append(ANY_SPEC)
    return pl.pallas_call(
        functools.partial(cut_kernel, at=at),
        in_specs=in_specs,
        out_specs=VMEM_SPEC,
        out_shape=pltpu.VMEM(shape, source.dtype),
        scratch_shapes=[pltpu.SemaphoreType.DMA],
        compiler_params=pltpu.CompilerParams(vmem_limit_bytes=KERNEL_VMEM),
        name="cut",
    )(*operands)


def chunk_sizes(head_count):
    tail = min(2, head_count // 2)
    return [1, head_count - 1 - tail, tail]


def replica_sum(value, axis):
    count = lax.axis_size(axis)
    if count & (count - 1):
        return lax.psum(value, axis)
    stride = 1
    while stride < count:
        value = value + lax.ppermute(value, axis, [(i, i ^ stride) for i in range(count)])
        stride *= 2
    return value


def body(stash, grad_out, doc_lengths):
    by_head = jnp.transpose(stash[0, 0], (1, 0, 2))
    head_count = by_head.shape[0]
    section_count = lax.axis_size("section")
    mirror = [(i, section_count - 1 - i) for i in range(section_count)]
    row_count = by_head.shape[1]
    split = row_count - row_count * 3 // 10 // ROW_TILE * ROW_TILE
    last = head_count - 1
    sizes = chunk_sizes(last)
    firsts = [sum(sizes[:i]) for i in range(len(sizes))]
    pieces = [(first, size, 0, row_count) for first, size in zip(firsts, sizes)]
    pieces += [(last, 1, 0, split), (last, 1, split, row_count - split)]
    grad_rows, lengths = grad_out[0, 0], doc_lengths[0, 0]
    arrived = []
    packed = None
    for head, heads, row, rows in pieces:
        packed = cut(by_head, (head, row, 0), (heads, rows, by_head.shape[2]), packed)
        arrived.append(lax.ppermute(packed, "section", mirror))
    grad_rows = cut(grad_rows, (0, 0), grad_rows.shape, packed)
    grads, bias, start_row = first_grads(*arrived[:2], grad_rows, lengths, head_count)
    bias_parts = [bias]
    for first, packed in zip(firsts[2:], arrived[2:]):
        grads, bias = chunk_grads(packed, grad_rows, start_row, first, grads)
        bias_parts.append(bias)
    early, late = arrived[-2:]
    query_early, sums, early_bias, mask = early_grads(
        early, grad_rows, start_row, last, bias_parts[-1]
    )
    query_late, added, bias_own = late_grads(early, late, grad_rows, mask, early_bias, bias_parts)
    bias_total = replica_sum(bias_own, "dp")
    grads = store_last((query_early, sums, query_late, added), grads)
    bias_grad = jnp.transpose(bias_total / lax.axis_size("dp"), (1, 0, 2))
    return (jnp.transpose(grads, (1, 0, 2))[None, None], bias_grad)


def solution(mesh):
    in_specs = (
        P("section", "dp", None, "tp", None),
        P("section", "dp", None, "tp"),
        P("section", "dp", None),
    )
    out_specs = (P("section", "dp", None, "tp", None), P("section", "tp", None))
    return jax.shard_map(body, mesh=mesh, in_specs=in_specs, out_specs=out_specs, check_vma=False)
```

```python
import functools
import math

import jax
import jax.numpy as jnp
from jax import lax
from jax.experimental import pallas as pl
from jax.experimental.pallas import tpu as pltpu
from jax.sharding import PartitionSpec as P

MASKED = -1e30
TILE = 128
ROW_TILE = 16
KERNEL_VMEM = 16 * 1024 * 1024


def doc_starts(lengths_ref, row_count):
    query_at = lax.broadcasted_iota(jnp.int32, (1, row_count), 1)
    doc_start = jnp.zeros((1, row_count), jnp.int32)
    doc_end = jnp.int32(0)
    for doc in range(lengths_ref.shape[0]):
        doc_end = doc_end + lengths_ref[doc]
        doc_start = jnp.where(query_at >= doc_end, doc_end, doc_start)
    return doc_start


ROWS_BY_ROWS = (((1,), (1,)), ((), ()))
PLAIN = (((1,), (0,)), ((), ()))
COLUMNS = (((0,), (0,)), ((), ()))
dot = functools.partial(lax.dot_general, preferred_element_type=jnp.float32)


def split_pack(packed):
    head_size = packed.shape[1] // 3
    return (
        packed[:, :head_size],
        packed[:, head_size : 2 * head_size],
        packed[:, 2 * head_size :],
    )


def mask_rows(doc_start, first_query, first_key, key_count):
    shape = (key_count, doc_start.shape[1])
    query_at = first_query + lax.broadcasted_iota(jnp.int32, (1, shape[1]), 1)
    key_at = first_key + lax.broadcasted_iota(jnp.int32, shape, 0)
    return jnp.where((key_at >= doc_start) & (key_at <= query_at), 0.0, MASKED)


def exponent_scale(head_size):
    return math.log2(math.e) / math.sqrt(head_size)


def low_weights(prob, prob_grad, head_size):
    prob_low = prob.astype(jnp.bfloat16)
    row_dot = jnp.sum(prob_low.astype(jnp.float32) * prob_grad, axis=0, keepdims=True)
    score_grad = (prob * (1.0 / math.sqrt(head_size))) * (prob_grad - row_dot)
    return prob_low, score_grad.astype(jnp.bfloat16)


def tile_weights(queries, keys_in, values_in, grad_rows, mask):
    head_size = queries.shape[1]
    masked = dot(keys_in, queries, ROWS_BY_ROWS) + mask
    row_top = jnp.max(masked, axis=0, keepdims=True)
    raised = jnp.exp2((masked - row_top) * exponent_scale(head_size))
    prob = raised * (1.0 / jnp.sum(raised, axis=0, keepdims=True))
    prob_grad = dot(values_in, grad_rows, ROWS_BY_ROWS)
    return low_weights(prob, prob_grad, head_size)


def head_grads(packed, grad_rows, doc_start):
    queries, keys_in, values_in = split_pack(packed)
    mask = mask_rows(doc_start, 0, 0, packed.shape[0])
    prob_low, score_low = tile_weights(queries, keys_in, values_in, grad_rows, mask)
    return (
        dot(score_low, keys_in, COLUMNS),
        dot(score_low, queries, PLAIN),
        dot(prob_low, grad_rows, PLAIN),
    )


def write_head(grads, out_ref, out_head, bias_ref, bias_head):
    for part, grad in enumerate(grads):
        head_size = grad.shape[1]
        span = slice(part * head_size, (part + 1) * head_size)
        out_ref[out_head, :, span] = grad.astype(jnp.bfloat16)
        bias_ref[bias_head, :, span] = jnp.sum(grad, axis=0, keepdims=True)


def chunk_kernel(packed_ref, grad_ref, start_ref, _mask, _grads, out_ref, bias_ref, *, first_head):
    head_size = packed_ref.shape[2] // 3
    head = pl.program_id(0)
    grad_at = pl.multiple_of((first_head + head) * head_size, head_size)
    grads = head_grads(packed_ref[head], grad_ref[:, pl.ds(grad_at, head_size)], start_ref[...])
    write_head(grads, out_ref, 0, bias_ref, head)


def first_kernel(lengths_ref, first_ref, rest_ref, grad_ref, out_ref, bias_ref, start_ref):
    head = pl.program_id(0)
    first_count = first_ref.shape[0]
    head_size = first_ref.shape[2] // 3

    @pl.when(head == 0)
    def _():
        start_ref[...] = doc_starts(lengths_ref, first_ref.shape[1])

    packed = jnp.where(
        head < first_count,
        first_ref[jnp.minimum(head, first_count - 1)],
        rest_ref[jnp.maximum(head - first_count, 0)],
    )
    grad_at = pl.multiple_of(head * head_size, head_size)
    grads = head_grads(packed, grad_ref[:, pl.ds(grad_at, head_size)], start_ref[...])
    write_head(grads, out_ref, 0, bias_ref, head)


def column_sum(rows):
    return jnp.sum(rows, axis=0, keepdims=True)


def mask_kernel(start_ref, mask_ref):
    key_count, query_count = mask_ref.shape
    row_count = start_ref.shape[1]
    first_query = row_count - query_count
    mask_ref[...] = mask_rows(
        start_ref[:, first_query:], first_query, row_count - key_count, key_count
    )


def early_kernel(
    early_ref, late_query_ref, grad_ref, start_ref, mask_ref, _,
    query_ref, sums_ref, bias_ref, raised_ref, prob_grad_ref, stats_ref, *, head
):
    row_count, pack_width = early_ref.shape[1:]
    head_size = pack_width // 3
    queries, keys_in, values_in = split_pack(early_ref[0])
    grad_rows = grad_ref[:row_count, head * head_size : (head + 1) * head_size]
    doc_start = start_ref[...]
    tiles = [slice(at, min(at + TILE, row_count)) for at in range(0, row_count, TILE)]
    key_grads, value_grads = [0.0] * len(tiles), [0.0] * len(tiles)
    query_bias = jnp.zeros((1, head_size), jnp.float32)
    for index, tile in enumerate(tiles):
        seen = slice(0, tile.stop)
        mask = mask_rows(doc_start[:, tile], tile.start, 0, tile.stop)
        prob_low, score_low = tile_weights(
            queries[tile], keys_in[seen], values_in[seen], grad_rows[tile], mask
        )
        query_grad = dot(score_low, keys_in[seen], COLUMNS)
        query_ref[tile] = query_grad.astype(jnp.bfloat16)
        query_bias += column_sum(query_grad)
        for past in range(index + 1):
            key_grads[past] += dot(score_low[tiles[past]], queries[tile], PLAIN)
            value_grads[past] += dot(prob_low[tiles[past]], grad_rows[tile], PLAIN)
    bias_ref[:, :head_size] = query_bias
    for part, grads in enumerate((key_grads, value_grads)):
        for tile, grad in zip(tiles, grads):
            sums_ref[tile, part * head_size : (part + 1) * head_size] = grad
        bias_ref[:, (part + 1) * head_size : (part + 2) * head_size] = sum(map(column_sum, grads))
    first_key = doc_start.shape[1] - mask_ref.shape[0]
    late_grad = grad_ref[row_count:, head * head_size : (head + 1) * head_size]
    masked = dot(keys_in[first_key:], late_query_ref[0], ROWS_BY_ROWS)
    masked += mask_ref[: row_count - first_key]
    row_top = jnp.max(masked, axis=0, keepdims=True)
    raised = jnp.exp2((masked - row_top) * exponent_scale(head_size))
    raised_ref[...] = raised
    prob_grad_ref[...] = dot(values_in[first_key:], late_grad, ROWS_BY_ROWS)
    stats_ref[0:1] = row_top
    stats_ref[1:2] = column_sum(raised)


def late_kernel(
    early_ref, late_query_ref, late_ref, grad_ref, mask_ref, raised_ref, prob_grad_ref, stats_ref,
    early_bias_ref, *refs
):
    bias_parts, (query_ref, added_ref, bias_ref) = refs[:-3], refs[-3:]
    split = early_ref.shape[1]
    early_keys = raised_ref.shape[0]
    first_key = split - early_keys
    head_size = early_ref.shape[2] // 3
    head = sum(part_ref.shape[0] for part_ref in bias_parts)
    queries = late_query_ref[0]
    grad_rows = grad_ref[split:, head * head_size : (head + 1) * head_size]
    late_keys = late_ref[0, :, :head_size]
    scale = exponent_scale(head_size)
    masked = dot(late_keys, queries, ROWS_BY_ROWS) + mask_ref[early_keys:]
    early_top = stats_ref[0:1]
    row_top = jnp.maximum(early_top, jnp.max(masked, axis=0, keepdims=True))
    raised = jnp.exp2((masked - row_top) * scale)
    lowered = jnp.exp2((early_top - row_top) * scale)
    inverse = 1.0 / (stats_ref[1:2] * lowered + column_sum(raised))
    prob = jnp.concatenate([raised_ref[...] * (lowered * inverse), raised * inverse], axis=0)
    prob_grad = jnp.concatenate(
        [prob_grad_ref[...], dot(late_ref[0, :, head_size:], grad_rows, ROWS_BY_ROWS)], axis=0
    )
    prob_low, score_low = low_weights(prob, prob_grad, head_size)
    keys_in = jnp.concatenate(
        [early_ref[0, first_key:, head_size : 2 * head_size], late_keys], axis=0
    )
    query_grad = dot(score_low, keys_in, COLUMNS)
    key_grad = dot(score_low, queries, PLAIN)
    value_grad = dot(prob_low, grad_rows, PLAIN)
    for part, grad in enumerate((query_grad, key_grad, value_grad)):
        span = slice(part * head_size, (part + 1) * head_size)
        bias_ref[head, :, span] = early_bias_ref[:, span] + column_sum(grad)
    query_ref[...] = query_grad.astype(jnp.bfloat16)
    added_ref[:, :head_size] = key_grad
    added_ref[:, head_size:] = value_grad
    head_at = 0
    for part_ref in bias_parts:
        bias_ref[head_at : head_at + part_ref.shape[0]] = part_ref[...]
        head_at += part_ref.shape[0]


def store_kernel(early_query_ref, sums_ref, late_query_ref, added_ref, _, out_ref, head_ref, semaphore):
    split, head_size = early_query_ref.shape
    first_key = head_ref.shape[1] - added_ref.shape[0]
    head_ref[0, :split, :head_size] = early_query_ref[...]
    head_ref[0, split:, :head_size] = late_query_ref[...]
    head_ref[0, :first_key, head_size:] = sums_ref[:first_key].astype(jnp.bfloat16)
    seen = split - first_key
    head_ref[0, first_key:split, head_size:] = (sums_ref[first_key:] + added_ref[:seen]).astype(
        jnp.bfloat16
    )
    head_ref[0, split:, head_size:] = added_ref[seen:].astype(jnp.bfloat16)
    at = out_ref.shape[0] - 1
    copy = pltpu.make_async_copy(head_ref, out_ref.at[pl.ds(at, 1)], semaphore)
    copy.start()
    copy.wait()


def in_vmem(array):
    return pltpu.with_memory_space_constraint(array, pltpu.VMEM)


VMEM_SPEC = pl.BlockSpec(memory_space=pltpu.VMEM)
SMEM_SPEC = pl.BlockSpec(memory_space=pltpu.SMEM)
ANY_SPEC = pl.BlockSpec(memory_space=pl.ANY)


def grads_outs(chunk_heads, head_count, first_head, row_count, pack_width):
    specs = [
        pl.BlockSpec((1, row_count, pack_width), lambda h: (first_head + h, 0, 0)),
        VMEM_SPEC,
    ]
    shapes = [
        jax.ShapeDtypeStruct((head_count, row_count, pack_width), jnp.bfloat16),
        pltpu.VMEM((chunk_heads, 1, pack_width), jnp.float32),
    ]
    return specs, shapes


def first_grads(first, rest, grad_rows, lengths, head_count):
    _, row_count, pack_width = first.shape
    chunk_heads = first.shape[0] + rest.shape[0]
    specs, shapes = grads_outs(chunk_heads, head_count, 0, row_count, pack_width)
    return pl.pallas_call(
        first_kernel,
        grid=(chunk_heads,),
        in_specs=[SMEM_SPEC, VMEM_SPEC, VMEM_SPEC, VMEM_SPEC],
        out_specs=specs + [VMEM_SPEC],
        out_shape=shapes + [pltpu.VMEM((1, row_count), jnp.int32)],
        compiler_params=pltpu.CompilerParams(vmem_limit_bytes=KERNEL_VMEM),
        name="first_grads",
    )(lengths, in_vmem(first), in_vmem(rest), in_vmem(grad_rows))


def chunk_grads(packed, grad_rows, start_row, mask, first_head, previous):
    chunk_heads, row_count, pack_width = packed.shape
    specs, shapes = grads_outs(chunk_heads, previous.shape[0], first_head, row_count, pack_width)
    return pl.pallas_call(
        functools.partial(chunk_kernel, first_head=first_head),
        grid=(chunk_heads,),
        in_specs=[VMEM_SPEC] * 4 + [ANY_SPEC],
        out_specs=specs,
        out_shape=shapes,
        input_output_aliases={4: 0},
        compiler_params=pltpu.CompilerParams(vmem_limit_bytes=KERNEL_VMEM),
    )(*map(in_vmem, (packed, grad_rows, start_row, mask)), previous)


def late_mask(start_row, split):
    row_count = start_row.shape[1]
    longest = row_count // 2
    first_key = max(0, split + 1 - longest) // ROW_TILE * ROW_TILE
    return pl.pallas_call(
        mask_kernel,
        in_specs=[VMEM_SPEC],
        out_specs=VMEM_SPEC,
        out_shape=pltpu.VMEM((row_count - first_key, row_count - split), jnp.float32),
        compiler_params=pltpu.CompilerParams(vmem_limit_bytes=KERNEL_VMEM),
        name="late_mask",
    )(in_vmem(start_row))


def early_grads(packed, late_queries, grad_rows, start_row, mask, head, after):
    _, split, pack_width = packed.shape
    head_size = pack_width // 3
    late_count = late_queries.shape[1]
    early_keys = mask.shape[0] - late_count
    operands = (packed, late_queries, grad_rows, start_row, mask, after)
    shapes = (
        ((split, head_size), jnp.bfloat16),
        ((split, 2 * head_size), jnp.float32),
        ((1, pack_width), jnp.float32),
        ((early_keys, late_count), jnp.float32),
        ((early_keys, late_count), jnp.float32),
        ((2, late_count), jnp.float32),
    )
    return pl.pallas_call(
        functools.partial(early_kernel, head=head),
        in_specs=[VMEM_SPEC] * len(operands),
        out_specs=[VMEM_SPEC] * len(shapes),
        out_shape=[pltpu.VMEM(*shape) for shape in shapes],
        compiler_params=pltpu.CompilerParams(vmem_limit_bytes=KERNEL_VMEM),
        name="early_grads",
    )(*map(in_vmem, operands))


def late_grads(early, late_queries, late, grad_rows, mask, started, early_bias, bias_parts):
    head_count = 1 + sum(part.shape[0] for part in bias_parts)
    pack_width = early.shape[2]
    head_size = pack_width // 3
    operands = [early, late_queries, late, grad_rows, mask, *started, early_bias, *bias_parts]
    return pl.pallas_call(
        late_kernel,
        in_specs=[VMEM_SPEC] * len(operands),
        out_specs=[VMEM_SPEC] * 3,
        out_shape=[
            pltpu.VMEM((late.shape[1], head_size), jnp.bfloat16),
            pltpu.VMEM((mask.shape[0], 2 * head_size), jnp.float32),
            pltpu.VMEM((head_count, 1, pack_width), jnp.float32),
        ],
        compiler_params=pltpu.CompilerParams(vmem_limit_bytes=KERNEL_VMEM),
        name="late_grads",
    )(*map(in_vmem, operands))


def store_last(parts, grads):
    return pl.pallas_call(
        store_kernel,
        in_specs=[VMEM_SPEC] * len(parts) + [ANY_SPEC],
        out_specs=ANY_SPEC,
        out_shape=jax.ShapeDtypeStruct(grads.shape, grads.dtype),
        scratch_shapes=[pltpu.VMEM((1, *grads.shape[1:]), grads.dtype), pltpu.SemaphoreType.DMA],
        input_output_aliases={len(parts): 0},
        compiler_params=pltpu.CompilerParams(vmem_limit_bytes=KERNEL_VMEM),
        name="store_last",
    )(*map(in_vmem, parts), grads)


def cut_kernel(source_ref, *refs, at):
    out_ref, semaphore = refs[-2:]
    window = tuple(pl.ds(start, size) for start, size in zip(at, out_ref.shape))
    copy = pltpu.make_async_copy(source_ref.at[window], out_ref, semaphore)
    copy.start()
    copy.wait()


def cut(source, at, shape, after):
    operands = [pltpu.with_memory_space_constraint(source, pltpu.HBM)]
    in_specs = [pl.BlockSpec(memory_space=pltpu.HBM)]
    if after is not None:
        operands.append(after)
        in_specs.append(ANY_SPEC)
    return pl.pallas_call(
        functools.partial(cut_kernel, at=at),
        in_specs=in_specs,
        out_specs=VMEM_SPEC,
        out_shape=pltpu.VMEM(shape, source.dtype),
        scratch_shapes=[pltpu.SemaphoreType.DMA],
        compiler_params=pltpu.CompilerParams(vmem_limit_bytes=KERNEL_VMEM),
        name="cut",
    )(*operands)


def chunk_sizes(head_count):
    tail = min(2, head_count // 2)
    return [1, head_count - 1 - tail, tail]


def replica_sum(value, axis):
    count = lax.axis_size(axis)
    if count & (count - 1):
        return lax.psum(value, axis)
    stride = 1
    while stride < count:
        value = value + lax.ppermute(value, axis, [(i, i ^ stride) for i in range(count)])
        stride *= 2
    return value


def body(stash, grad_out, doc_lengths):
    by_head = jnp.transpose(stash[0, 0], (1, 0, 2))
    head_count = by_head.shape[0]
    section_count = lax.axis_size("section")
    mirror = [(i, section_count - 1 - i) for i in range(section_count)]
    row_count = by_head.shape[1]
    split = row_count - TILE
    last = head_count - 1
    sizes = chunk_sizes(last)
    firsts = [sum(sizes[:i]) for i in range(len(sizes))]
    pack_width = by_head.shape[2]
    head_size = pack_width // 3
    late_count = row_count - split
    pieces = [
        ((first, 0, 0), (size, row_count, pack_width)) for first, size in zip(firsts, sizes)
    ]
    pieces += [
        ((last, split, 0), (1, late_count, head_size)),
        ((last, 0, 0), (1, split, pack_width)),
        ((last, split, head_size), (1, late_count, pack_width - head_size)),
    ]
    grad_rows, lengths = grad_out[0, 0], doc_lengths[0, 0]
    arrived = []
    packed = None
    for at, shape in pieces:
        packed = cut(by_head, at, shape, packed)
        arrived.append(lax.ppermute(packed, "section", mirror))
    grad_rows = cut(grad_rows, (0, 0), grad_rows.shape, packed)
    grads, bias, start_row = first_grads(*arrived[:2], grad_rows, lengths, head_count)
    mask = late_mask(start_row, split)
    bias_parts = [bias]
    for first, packed in zip(firsts[2:], arrived[2:-3]):
        grads, bias = chunk_grads(packed, grad_rows, start_row, mask, first, grads)
        bias_parts.append(bias)
    late_queries, early, late = arrived[-3:]
    query_early, sums, early_bias, *started = early_grads(
        early, late_queries, grad_rows, start_row, mask, last, bias_parts[-1]
    )
    query_late, added, bias_own = late_grads(
        early, late_queries, late, grad_rows, mask, started, early_bias, bias_parts
    )
    bias_total = replica_sum(bias_own, "dp")
    grads = store_last((query_early, sums, query_late, added), grads)
    bias_grad = jnp.transpose(bias_total / lax.axis_size("dp"), (1, 0, 2))
    return (jnp.transpose(grads, (1, 0, 2))[None, None], bias_grad)


def solution(mesh):
    in_specs = (
        P("section", "dp", None, "tp", None),
        P("section", "dp", None, "tp"),
        P("section", "dp", None),
    )
    out_specs = (P("section", "dp", None, "tp", None), P("section", "tp", None))
    return jax.shard_map(body, mesh=mesh, in_specs=in_specs, out_specs=out_specs, check_vma=False)
```

```python
import functools
import math

import jax
import jax.numpy as jnp
from jax import lax
from jax.experimental import pallas as pl
from jax.experimental.pallas import tpu as pltpu
from jax.sharding import PartitionSpec as P

MASKED = -1e30
TILE = 128
ROW_TILE = 16
KERNEL_VMEM = 16 * 1024 * 1024


def doc_starts(lengths_ref, row_count):
    query_at = lax.broadcasted_iota(jnp.int32, (1, row_count), 1)
    doc_start = jnp.zeros((1, row_count), jnp.int32)
    doc_end = jnp.int32(0)
    for doc in range(lengths_ref.shape[0]):
        doc_end = doc_end + lengths_ref[doc]
        doc_start = jnp.where(query_at >= doc_end, doc_end, doc_start)
    return doc_start


ROWS_BY_ROWS = (((1,), (1,)), ((), ()))
PLAIN = (((1,), (0,)), ((), ()))
COLUMNS = (((0,), (0,)), ((), ()))
dot = functools.partial(lax.dot_general, preferred_element_type=jnp.float32)


def split_pack(packed):
    head_size = packed.shape[1] // 3
    return (
        packed[:, :head_size],
        packed[:, head_size : 2 * head_size],
        packed[:, 2 * head_size :],
    )


def mask_rows(doc_start, first_query, first_key, key_count):
    shape = (key_count, doc_start.shape[1])
    query_at = first_query + lax.broadcasted_iota(jnp.int32, (1, shape[1]), 1)
    key_at = first_key + lax.broadcasted_iota(jnp.int32, shape, 0)
    return jnp.where((key_at >= doc_start) & (key_at <= query_at), 0.0, MASKED)


def exponent_scale(head_size):
    return math.log2(math.e) / math.sqrt(head_size)


def low_weights(prob, prob_grad, head_size):
    prob_low = prob.astype(jnp.bfloat16)
    row_dot = jnp.sum(prob_low.astype(jnp.float32) * prob_grad, axis=0, keepdims=True)
    score_grad = (prob * (1.0 / math.sqrt(head_size))) * (prob_grad - row_dot)
    return prob_low, score_grad.astype(jnp.bfloat16)


def tile_weights(queries, keys_in, values_in, grad_rows, mask):
    head_size = queries.shape[1]
    masked = dot(keys_in, queries, ROWS_BY_ROWS) + mask
    row_top = jnp.max(masked, axis=0, keepdims=True)
    raised = jnp.exp2((masked - row_top) * exponent_scale(head_size))
    prob = raised * (1.0 / jnp.sum(raised, axis=0, keepdims=True))
    prob_grad = dot(values_in, grad_rows, ROWS_BY_ROWS)
    return low_weights(prob, prob_grad, head_size)


def head_grads(packed, grad_rows, doc_start):
    queries, keys_in, values_in = split_pack(packed)
    mask = mask_rows(doc_start, 0, 0, packed.shape[0])
    prob_low, score_low = tile_weights(queries, keys_in, values_in, grad_rows, mask)
    return (
        dot(score_low, keys_in, COLUMNS),
        dot(score_low, queries, PLAIN),
        dot(prob_low, grad_rows, PLAIN),
    )


def write_head(grads, out_ref, out_head, bias_ref, bias_head):
    for part, grad in enumerate(grads):
        head_size = grad.shape[1]
        span = slice(part * head_size, (part + 1) * head_size)
        out_ref[out_head, :, span] = grad.astype(jnp.bfloat16)
        bias_ref[bias_head, :, span] = jnp.sum(grad, axis=0, keepdims=True)


def chunk_kernel(packed_ref, grad_ref, start_ref, _mask, _grads, out_ref, bias_ref, *, first_head):
    head_size = packed_ref.shape[2] // 3
    head = pl.program_id(0)
    grad_at = pl.multiple_of((first_head + head) * head_size, head_size)
    grads = head_grads(packed_ref[head], grad_ref[:, pl.ds(grad_at, head_size)], start_ref[...])
    write_head(grads, out_ref, 0, bias_ref, head)


def first_kernel(lengths_ref, first_ref, rest_ref, grad_ref, out_ref, bias_ref, start_ref):
    head = pl.program_id(0)
    first_count = first_ref.shape[0]
    head_size = first_ref.shape[2] // 3

    @pl.when(head == 0)
    def _():
        start_ref[...] = doc_starts(lengths_ref, first_ref.shape[1])

    packed = jnp.where(
        head < first_count,
        first_ref[jnp.minimum(head, first_count - 1)],
        rest_ref[jnp.maximum(head - first_count, 0)],
    )
    grad_at = pl.multiple_of(head * head_size, head_size)
    grads = head_grads(packed, grad_ref[:, pl.ds(grad_at, head_size)], start_ref[...])
    write_head(grads, out_ref, 0, bias_ref, head)


def column_sum(rows):
    return jnp.sum(rows, axis=0, keepdims=True)


def mask_kernel(start_ref, mask_ref):
    key_count, query_count = mask_ref.shape
    row_count = start_ref.shape[1]
    first_query = row_count - query_count
    mask_ref[...] = mask_rows(
        start_ref[:, first_query:], first_query, row_count - key_count, key_count
    )


def opening_kernel(packed_ref, grad_ref, start_ref, _, query_ref, sums_ref, bias_ref, *, head):
    row_count, pack_width = packed_ref.shape[1:]
    head_size = pack_width // 3
    grad_rows = grad_ref[:row_count, head * head_size : (head + 1) * head_size]
    grads = head_grads(packed_ref[0], grad_rows, start_ref[:, :row_count])
    query_ref[...] = grads[0].astype(jnp.bfloat16)
    for part, grad in enumerate(grads):
        bias_ref[:, part * head_size : (part + 1) * head_size] = column_sum(grad)
        if part:
            sums_ref[:, (part - 1) * head_size : part * head_size] = grad


def early_kernel(
    opening_ref, early_ref, late_query_ref, grad_ref, start_ref, mask_ref, query_ref, sums_ref,
    bias_ref, query_out, sums_out, bias_out, raised_ref, prob_grad_ref, stats_ref, *, head
):
    head_size = early_ref.shape[2] // 3
    begin = opening_ref.shape[1]
    split = begin + early_ref.shape[1]
    queries = early_ref[0, :, :head_size]
    keys_in, values_in = (
        jnp.concatenate([opening_ref[0, :, span], early_ref[0, :, span]], axis=0)
        for span in (slice(head_size, 2 * head_size), slice(2 * head_size, None))
    )
    grad_span = slice(head * head_size, (head + 1) * head_size)
    grad_rows = grad_ref[begin:split, grad_span]
    mask = mask_rows(start_ref[:, begin:split], begin, 0, split)
    prob_low, score_low = tile_weights(queries, keys_in, values_in, grad_rows, mask)
    first_key = start_ref.shape[1] - mask_ref.shape[0]
    masked = dot(keys_in[first_key:], late_query_ref[0], ROWS_BY_ROWS)
    masked += mask_ref[: split - first_key]
    row_top = jnp.max(masked, axis=0, keepdims=True)
    raised = jnp.exp2((masked - row_top) * exponent_scale(head_size))
    raised_ref[...] = raised
    prob_grad_ref[...] = dot(values_in[first_key:], grad_ref[split:, grad_span], ROWS_BY_ROWS)
    stats_ref[0:1] = row_top
    stats_ref[1:2] = column_sum(raised)
    query_grad = dot(score_low, keys_in, COLUMNS)
    query_out[:begin] = query_ref[...]
    query_out[begin:] = query_grad.astype(jnp.bfloat16)
    bias_out[:, :head_size] = bias_ref[:, :head_size] + column_sum(query_grad)
    added = (dot(score_low, queries, PLAIN), dot(prob_low, grad_rows, PLAIN))
    for part, grad in enumerate(added):
        span = slice(part * head_size, (part + 1) * head_size)
        bias_span = slice((part + 1) * head_size, (part + 2) * head_size)
        sums_out[:begin, span] = sums_ref[:, span] + grad[:begin]
        sums_out[begin:, span] = grad[begin:]
        bias_out[:, bias_span] = bias_ref[:, bias_span] + column_sum(grad)


def late_kernel(
    opening_ref, early_ref, late_query_ref, late_ref, grad_ref, mask_ref, raised_ref, prob_grad_ref,
    stats_ref, early_bias_ref, *refs
):
    bias_parts, (query_ref, added_ref, bias_ref) = refs[:-3], refs[-3:]
    begin = opening_ref.shape[1]
    split = begin + early_ref.shape[1]
    early_keys = raised_ref.shape[0]
    first_key = split - early_keys
    head_size = early_ref.shape[2] // 3
    head = sum(part_ref.shape[0] for part_ref in bias_parts)
    queries = late_query_ref[0]
    grad_rows = grad_ref[split:, head * head_size : (head + 1) * head_size]
    late_keys = late_ref[0, :, :head_size]
    scale = exponent_scale(head_size)
    masked = dot(late_keys, queries, ROWS_BY_ROWS) + mask_ref[early_keys:]
    early_top = stats_ref[0:1]
    row_top = jnp.maximum(early_top, jnp.max(masked, axis=0, keepdims=True))
    raised = jnp.exp2((masked - row_top) * scale)
    lowered = jnp.exp2((early_top - row_top) * scale)
    inverse = 1.0 / (stats_ref[1:2] * lowered + column_sum(raised))
    prob = jnp.concatenate([raised_ref[...] * (lowered * inverse), raised * inverse], axis=0)
    prob_grad = jnp.concatenate(
        [prob_grad_ref[...], dot(late_ref[0, :, head_size:], grad_rows, ROWS_BY_ROWS)], axis=0
    )
    prob_low, score_low = low_weights(prob, prob_grad, head_size)
    keys_in = jnp.concatenate(
        [
            opening_ref[0, first_key:, head_size : 2 * head_size],
            early_ref[0, :, head_size : 2 * head_size],
            late_keys,
        ],
        axis=0,
    )
    query_grad = dot(score_low, keys_in, COLUMNS)
    key_grad = dot(score_low, queries, PLAIN)
    value_grad = dot(prob_low, grad_rows, PLAIN)
    for part, grad in enumerate((query_grad, key_grad, value_grad)):
        span = slice(part * head_size, (part + 1) * head_size)
        bias_ref[head, :, span] = early_bias_ref[:, span] + column_sum(grad)
    query_ref[...] = query_grad.astype(jnp.bfloat16)
    added_ref[:, :head_size] = key_grad
    added_ref[:, head_size:] = value_grad
    head_at = 0
    for part_ref in bias_parts:
        bias_ref[head_at : head_at + part_ref.shape[0]] = part_ref[...]
        head_at += part_ref.shape[0]


def store_kernel(early_query_ref, sums_ref, late_query_ref, added_ref, _, out_ref, head_ref, semaphore):
    split, head_size = early_query_ref.shape
    first_key = head_ref.shape[1] - added_ref.shape[0]
    head_ref[0, :split, :head_size] = early_query_ref[...]
    head_ref[0, split:, :head_size] = late_query_ref[...]
    head_ref[0, :first_key, head_size:] = sums_ref[:first_key].astype(jnp.bfloat16)
    seen = split - first_key
    head_ref[0, first_key:split, head_size:] = (sums_ref[first_key:] + added_ref[:seen]).astype(
        jnp.bfloat16
    )
    head_ref[0, split:, head_size:] = added_ref[seen:].astype(jnp.bfloat16)
    at = out_ref.shape[0] - 1
    copy = pltpu.make_async_copy(head_ref, out_ref.at[pl.ds(at, 1)], semaphore)
    copy.start()
    copy.wait()


def in_vmem(array):
    return pltpu.with_memory_space_constraint(array, pltpu.VMEM)


VMEM_SPEC = pl.BlockSpec(memory_space=pltpu.VMEM)
SMEM_SPEC = pl.BlockSpec(memory_space=pltpu.SMEM)
ANY_SPEC = pl.BlockSpec(memory_space=pl.ANY)


def grads_outs(chunk_heads, head_count, first_head, row_count, pack_width):
    specs = [
        pl.BlockSpec((1, row_count, pack_width), lambda h: (first_head + h, 0, 0)),
        VMEM_SPEC,
    ]
    shapes = [
        jax.ShapeDtypeStruct((head_count, row_count, pack_width), jnp.bfloat16),
        pltpu.VMEM((chunk_heads, 1, pack_width), jnp.float32),
    ]
    return specs, shapes


def first_grads(first, rest, grad_rows, lengths, head_count):
    _, row_count, pack_width = first.shape
    chunk_heads = first.shape[0] + rest.shape[0]
    specs, shapes = grads_outs(chunk_heads, head_count, 0, row_count, pack_width)
    return pl.pallas_call(
        first_kernel,
        grid=(chunk_heads,),
        in_specs=[SMEM_SPEC, VMEM_SPEC, VMEM_SPEC, VMEM_SPEC],
        out_specs=specs + [VMEM_SPEC],
        out_shape=shapes + [pltpu.VMEM((1, row_count), jnp.int32)],
        compiler_params=pltpu.CompilerParams(vmem_limit_bytes=KERNEL_VMEM),
        name="first_grads",
    )(lengths, in_vmem(first), in_vmem(rest), in_vmem(grad_rows))


def chunk_grads(packed, grad_rows, start_row, mask, first_head, previous):
    chunk_heads, row_count, pack_width = packed.shape
    specs, shapes = grads_outs(chunk_heads, previous.shape[0], first_head, row_count, pack_width)
    return pl.pallas_call(
        functools.partial(chunk_kernel, first_head=first_head),
        grid=(chunk_heads,),
        in_specs=[VMEM_SPEC] * 4 + [ANY_SPEC],
        out_specs=specs,
        out_shape=shapes,
        input_output_aliases={4: 0},
        compiler_params=pltpu.CompilerParams(vmem_limit_bytes=KERNEL_VMEM),
    )(*map(in_vmem, (packed, grad_rows, start_row, mask)), previous)


def late_mask(start_row, split):
    row_count = start_row.shape[1]
    longest = row_count // 2
    first_key = max(0, split + 1 - longest) // ROW_TILE * ROW_TILE
    return pl.pallas_call(
        mask_kernel,
        in_specs=[VMEM_SPEC],
        out_specs=VMEM_SPEC,
        out_shape=pltpu.VMEM((row_count - first_key, row_count - split), jnp.float32),
        compiler_params=pltpu.CompilerParams(vmem_limit_bytes=KERNEL_VMEM),
        name="late_mask",
    )(in_vmem(start_row))


def vmem_call(kernel, operands, shapes):
    return pl.pallas_call(
        kernel,
        in_specs=[VMEM_SPEC] * len(operands),
        out_specs=[VMEM_SPEC] * len(shapes),
        out_shape=[pltpu.VMEM(*shape) for shape in shapes],
        compiler_params=pltpu.CompilerParams(vmem_limit_bytes=KERNEL_VMEM),
    )(*map(in_vmem, operands))


def grad_shapes(rows, pack_width):
    head_size = pack_width // 3
    return (
        ((rows, head_size), jnp.bfloat16),
        ((rows, 2 * head_size), jnp.float32),
        ((1, pack_width), jnp.float32),
    )


def opening_grads(packed, grad_rows, start_row, head, after):
    return vmem_call(
        functools.partial(opening_kernel, head=head),
        (packed, grad_rows, start_row, after),
        grad_shapes(*packed.shape[1:]),
    )


def early_grads(opening, packed, late_queries, grad_rows, start_row, mask, opened, head):
    split = opening.shape[1] + packed.shape[1]
    late_count = late_queries.shape[1]
    tile = (mask.shape[0] - late_count, late_count)
    shapes = grad_shapes(split, packed.shape[2])
    shapes += ((tile, jnp.float32), (tile, jnp.float32), ((2, late_count), jnp.float32))
    operands = (opening, packed, late_queries, grad_rows, start_row, mask, *opened)
    return vmem_call(functools.partial(early_kernel, head=head), operands, shapes)


def late_grads(opening, early, late_queries, late, grad_rows, mask, started, early_bias, bias_parts):
    head_count = 1 + sum(part.shape[0] for part in bias_parts)
    pack_width = early.shape[2]
    head_size = pack_width // 3
    operands = [opening, early, late_queries, late, grad_rows, mask, *started, early_bias, *bias_parts]
    return pl.pallas_call(
        late_kernel,
        in_specs=[VMEM_SPEC] * len(operands),
        out_specs=[VMEM_SPEC] * 3,
        out_shape=[
            pltpu.VMEM((late.shape[1], head_size), jnp.bfloat16),
            pltpu.VMEM((mask.shape[0], 2 * head_size), jnp.float32),
            pltpu.VMEM((head_count, 1, pack_width), jnp.float32),
        ],
        compiler_params=pltpu.CompilerParams(vmem_limit_bytes=KERNEL_VMEM),
        name="late_grads",
    )(*map(in_vmem, operands))


def store_last(parts, grads):
    return pl.pallas_call(
        store_kernel,
        in_specs=[VMEM_SPEC] * len(parts) + [ANY_SPEC],
        out_specs=ANY_SPEC,
        out_shape=jax.ShapeDtypeStruct(grads.shape, grads.dtype),
        scratch_shapes=[pltpu.VMEM((1, *grads.shape[1:]), grads.dtype), pltpu.SemaphoreType.DMA],
        input_output_aliases={len(parts): 0},
        compiler_params=pltpu.CompilerParams(vmem_limit_bytes=KERNEL_VMEM),
        name="store_last",
    )(*map(in_vmem, parts), grads)


def cut_kernel(source_ref, *refs, at):
    out_ref, semaphore = refs[-2:]
    window = tuple(pl.ds(start, size) for start, size in zip(at, out_ref.shape))
    copy = pltpu.make_async_copy(source_ref.at[window], out_ref, semaphore)
    copy.start()
    copy.wait()


def cut(source, at, shape, after):
    operands = [pltpu.with_memory_space_constraint(source, pltpu.HBM)]
    in_specs = [pl.BlockSpec(memory_space=pltpu.HBM)]
    if after is not None:
        operands.append(after)
        in_specs.append(ANY_SPEC)
    return pl.pallas_call(
        functools.partial(cut_kernel, at=at),
        in_specs=in_specs,
        out_specs=VMEM_SPEC,
        out_shape=pltpu.VMEM(shape, source.dtype),
        scratch_shapes=[pltpu.SemaphoreType.DMA],
        compiler_params=pltpu.CompilerParams(vmem_limit_bytes=KERNEL_VMEM),
        name="cut",
    )(*operands)


def chunk_sizes(head_count):
    tail = min(2, head_count // 2)
    return [1, head_count - 1 - tail, tail]


def replica_sum(value, axis):
    count = lax.axis_size(axis)
    if count & (count - 1):
        return lax.psum(value, axis)
    stride = 1
    while stride < count:
        value = value + lax.ppermute(value, axis, [(i, i ^ stride) for i in range(count)])
        stride *= 2
    return value


def body(stash, grad_out, doc_lengths):
    by_head = jnp.transpose(stash[0, 0], (1, 0, 2))
    head_count = by_head.shape[0]
    section_count = lax.axis_size("section")
    mirror = [(i, section_count - 1 - i) for i in range(section_count)]
    row_count = by_head.shape[1]
    split = row_count - row_count * 3 // 10 // ROW_TILE * ROW_TILE
    last = head_count - 1
    sizes = chunk_sizes(last)
    firsts = [sum(sizes[:i]) for i in range(len(sizes))]
    pack_width = by_head.shape[2]
    head_size = pack_width // 3
    late_count = row_count - split
    pieces = [
        ((first, 0, 0), (size, row_count, pack_width)) for first, size in zip(firsts, sizes)
    ]
    pieces += [
        ((last, 0, 0), (1, TILE, pack_width)),
        ((last, split, 0), (1, late_count, head_size)),
        ((last, TILE, 0), (1, split - TILE, pack_width)),
        ((last, split, head_size), (1, late_count, pack_width - head_size)),
    ]
    grad_rows, lengths = grad_out[0, 0], doc_lengths[0, 0]
    arrived = []
    packed = None
    for at, shape in pieces:
        packed = cut(by_head, at, shape, packed)
        arrived.append(lax.ppermute(packed, "section", mirror))
    grad_rows = cut(grad_rows, (0, 0), grad_rows.shape, packed)
    grads, bias, start_row = first_grads(*arrived[:2], grad_rows, lengths, head_count)
    mask = late_mask(start_row, split)
    bias_parts = [bias]
    for first, packed in zip(firsts[2:], arrived[2:-4]):
        grads, bias = chunk_grads(packed, grad_rows, start_row, mask, first, grads)
        bias_parts.append(bias)
    opening, late_queries, early, late = arrived[-4:]
    opened = opening_grads(opening, grad_rows, start_row, last, bias_parts[-1])
    query_early, sums, early_bias, *started = early_grads(
        opening, early, late_queries, grad_rows, start_row, mask, opened, last
    )
    query_late, added, bias_own = late_grads(
        opening, early, late_queries, late, grad_rows, mask, started, early_bias, bias_parts
    )
    bias_total = replica_sum(bias_own, "dp")
    grads = store_last((query_early, sums, query_late, added), grads)
    bias_grad = jnp.transpose(bias_total / lax.axis_size("dp"), (1, 0, 2))
    return (jnp.transpose(grads, (1, 0, 2))[None, None], bias_grad)


def solution(mesh):
    in_specs = (
        P("section", "dp", None, "tp", None),
        P("section", "dp", None, "tp"),
        P("section", "dp", None),
    )
    out_specs = (P("section", "dp", None, "tp", None), P("section", "tp", None))
    return jax.shard_map(body, mesh=mesh, in_specs=in_specs, out_specs=out_specs, check_vma=False)
```
